32 devices in a mesh: fsdp: 2 (over y), ctx: 4 (over x, core), tp: 4 (over z).
Axes of the slice: x: 2, y: 2, z: 4, core: 2. Of those that a mesh axis runs over, the one named last changes fastest.
Arguments:
- tokens: bfloat16 [2, 2048, 2048], P('fsdp', 'ctx'), may hold values from -6 to 6
- q_weight: bfloat16 [2048, 2048], P(('fsdp', 'ctx'), 'tp'), may hold values from -0.125 to 0.125
- k_weight: bfloat16 [2048, 2048], P(('fsdp', 'ctx'), 'tp'), may hold values from -0.125 to 0.125
- v_weight: bfloat16 [2048, 2048], P(('fsdp', 'ctx'), 'tp'), may hold values from -0.125 to 0.125
- o_weight: bfloat16 [2048, 2048], P(('fsdp', 'ctx'), 'tp'), may hold values from -0.125 to 0.125
- gate_weight: bfloat16 [2048, 8192], P(('fsdp', 'ctx'), 'tp'), may hold values from -0.125 to 0.125
- up_weight: bfloat16 [2048, 8192], P(('fsdp', 'ctx'), 'tp'), may hold values from -0.125 to 0.125
- down_weight: bfloat16 [2048, 8192], P(('fsdp', 'ctx'), 'tp'), may hold values from -0.0625 to 0.0625
- norm_gains: bfloat16 [2048, 4], P(('fsdp', 'ctx')), may hold values from 0.5 to 2
- cotangent: bfloat16 [2, 2048, 2048], P('fsdp', 'ctx'), may hold values from -6 to 6
Outputs:
- block_out: bfloat16 [2, 2048, 2048], P('fsdp', 'ctx')
- token_grad: float32 [2, 2048, 2048], P('fsdp', 'ctx')
- q_grad: float32 [2048, 2048], P(('fsdp', 'ctx'), 'tp')
- k_grad: float32 [2048, 2048], P(('fsdp', 'ctx'), 'tp')
- v_grad: float32 [2048, 2048], P(('fsdp', 'ctx'), 'tp')
- o_grad: float32 [2048, 2048], P(('fsdp', 'ctx'), 'tp')
- gate_grad: float32 [2048, 8192], P(('fsdp', 'ctx'), 'tp')
- up_grad: float32 [2048, 8192], P(('fsdp', 'ctx'), 'tp')
- down_grad: float32 [2048, 8192], P(('fsdp', 'ctx'), 'tp')
- gain_grad: float32 [2048, 4], P(('fsdp', 'ctx'))
The draws below stay inside these ranges and needn't reach their ends.
All inputs are finite; a program needn't handle non-finite values.
Results may differ from the reference program's by a relative error of at most 0.017.
Values may be sent and summed in bfloat16 or wider, within the bound.
No kernel may reach another device: no remote copies, remote signals or barrier semaphores. Data moves between devices by JAX's collectives and lax.ppermute only.
A program may use at most 192 MiB of HBM per device.

```python
import math
import jax
import jax.numpy as jnp
from jax import lax

D = 2048
HEADS = 16
HEAD_DIM = 128
FF = 8192
SEQ_LEN = 2048
SEQS = 2


def raised(values, own_key, source, target, shards_of, factor):
    owner, partner = [(jnp.arange(values.shape[dim]) // (values.shape[dim] // shards_of)).reshape([-1 if axis == dim else 1 for axis in range(values.ndim)]) for dim in (source, target)]
    chosen = jax.random.permutation(own_key, shards_of)[partner]
    strong = (owner == chosen) | (owner == (partner + shards_of // 2) % shards_of)
    return jnp.where(strong, factor * values, values)


def block_scale(key, shape, cuts, least, top_value):
    loudness, own = 1.0, jax.random.fold_in(key, 6)
    for dim, shards_of in cuts:
        draws = jnp.exp(jax.random.uniform(jax.random.fold_in(own, dim), (shards_of,), jnp.float32, least / len(cuts), top_value / len(cuts)))
        loudness = loudness * jnp.repeat(draws, shape[dim] // shards_of).reshape([-1 if axis == dim else 1 for axis in range(len(shape))])
    return loudness


def scatter_about(own_key, extent, width, most, split=(), held_as=jnp.bfloat16):
    result = jax.random.normal(own_key, extent, jnp.float32) * width
    if len(split) > 0:
        result = block_scale(own_key, extent, split, -0.22, 0.18) * result
    return jnp.clip(result, min=-most, max=most).astype(held_as)


def bell_draw_with(own_key, dims, width, most, pieces, heavy, held_as=jnp.bfloat16):
    result = width * jax.random.normal(own_key, dims, jnp.float32)
    if pieces:
        result = result * block_scale(own_key, dims, pieces, -0.22, 0.18)
    return jnp.clip(raised(result, jax.random.fold_in(own_key, 3), *heavy), -most, most).astype(held_as)


def setup_inputs(seed: int = 0) -> dict:
    splits = jax.random.split(jax.random.key(seed), 11)
    tokens = bell_draw_with(splits[0], (SEQS, SEQ_LEN, D), 1.0, 6.0, ((0, 2), (1, 4)), (1, 2, 4, 2.0))
    q_weight = scatter_about(splits[1], (D, D), D ** -0.5, 0.125, ((0, 8), (1, 4)))
    k_weight = scatter_about(splits[2], (D, D), D ** -0.5, 0.125, ((0, 8), (1, 4)))
    v_weight = scatter_about(splits[3], (D, D), D ** -0.5, 0.125, ((0, 8), (1, 4)))
    o_weight = scatter_about(splits[4], (D, D), D ** -0.5, 0.125, ((0, 8), (1, 4)))
    gate_weight = scatter_about(splits[5], (D, FF), D ** -0.5, 0.125, ((0, 8), (1, 4)))
    up_weight = scatter_about(splits[6], (D, FF), D ** -0.5, 0.125, ((0, 8), (1, 4)))
    down_weight = scatter_about(splits[7], (D, FF), FF ** -0.5, 0.0625, ((0, 8), (1, 4)))
    norm_gains = jnp.clip(0.5 + 1.5 * jax.random.uniform(splits[8], (D, 4), jnp.float32) ** block_scale(splits[8], (D, 4), ((0, 8),), -0.2, 0.2), 0.5, 2.0).astype(jnp.bfloat16)
    cotangent = bell_draw_with(splits[9], (SEQS, SEQ_LEN, D), 1.0, 6.0, ((0, 2), (1, 4)), (0, 2, 2, 2.0))
    return dict(tokens=tokens, q_weight=q_weight, k_weight=k_weight, v_weight=v_weight, o_weight=o_weight, gate_weight=gate_weight, up_weight=up_weight, down_weight=down_weight, norm_gains=norm_gains, cotangent=cotangent)


@jax.custom_vjp
def low(v):
    return lax.optimization_barrier(v.astype(jnp.bfloat16)).astype(jnp.float32)

@jax.custom_vjp
def low_back(v):
    return v

def low_keep(v):
    return (low(v), None)

def low_pass(kept, grad):
    return (grad,)

def back_keep(v):
    return (v, None)

def back_low(kept, grad):
    return (low(grad),)
low.defvjp(low_keep, low_pass)
low_back.defvjp(back_keep, back_low)
highest = lax.Precision.HIGHEST
norm_eps = 1e-06
rope_base = 500000.0

def matmul(left, right):
    return jnp.dot(left, right, precision=highest)

def matmul_t(left, right):
    return jnp.dot(left, right.T, precision=highest)

def rms_scale(values_in):
    return lax.rsqrt(lax.optimization_barrier(jnp.mean(values_in * values_in, axis=-1, keepdims=True)) + norm_eps)

def rope_tables(length, offset):
    half_dim = HEAD_DIM // 2
    frequency = rope_base ** (-(jnp.arange(half_dim, dtype=jnp.float32) * 2.0) / HEAD_DIM)
    angles = (offset + jnp.arange(length, dtype=jnp.int32)).astype(jnp.float32)[:, None] * frequency[None, :]
    return (jnp.cos(angles), jnp.sin(angles))

def rotate(values_in, cosine_table, sine_table):
    half_dim = values_in.shape[-1] // 2
    first_half = values_in[..., :half_dim]
    second_half = values_in[..., half_dim:]
    cosine = cosine_table[:, None, :]
    sine_part = sine_table[:, None, :]
    return jnp.concatenate([first_half * cosine - second_half * sine_part, second_half * cosine + first_half * sine_part], axis=-1)

def attend_block(query_block, start, keys, values):
    block_rows = query_block.shape[0]
    length = keys.shape[0]
    scores = jnp.einsum('qhd,khd->hqk', query_block, keys, precision=highest) * (1.0 / math.sqrt(HEAD_DIM))
    scores = low_back(scores)
    query_pos = start + jnp.arange(block_rows, dtype=jnp.int32)
    key_pos = jnp.arange(length, dtype=jnp.int32)
    allowed = key_pos[None, :] <= query_pos[:, None]
    scores = jnp.where(allowed[None], scores, -1e+30)
    row_max = lax.optimization_barrier(jnp.max(scores, axis=-1, keepdims=True))
    weights = jnp.exp(scores - row_max)
    probs = weights / lax.optimization_barrier(jnp.sum(weights, axis=-1, keepdims=True))
    probs = low(probs)
    return jnp.einsum('hqk,khd->qhd', probs, values, precision=highest)

def attention(q_rot, k_rot, v_low):
    length = q_rot.shape[0]
    block_rows = min(512, length)
    block_count = length // block_rows
    query_blocks = q_rot.reshape(block_count, block_rows, HEADS, HEAD_DIM)
    starts = jnp.arange(block_count, dtype=jnp.int32) * block_rows

    def one_block(packed):
        return attend_block(packed[0], packed[1], k_rot, v_low)
    attended = lax.map(jax.checkpoint(one_block), (query_blocks, starts))
    return attended.reshape(length, HEADS * HEAD_DIM)

def sequence_forward(inputs, w_query, w_key, w_value, w_out, w_gate, w_up, w_down, gain_table):
    length = inputs.shape[0]
    q_proj = low_back(matmul(inputs, w_query))
    k_proj = low_back(matmul(inputs, w_key))
    v_proj = low(low_back(matmul(inputs, w_value)))
    q_norm = q_proj * rms_scale(q_proj) * gain_table[:, 0]
    k_norm = k_proj * rms_scale(k_proj) * gain_table[:, 1]
    cosine_table, sine_table = rope_tables(length, 0)
    q_rot = low(rotate(q_norm.reshape(length, HEADS, HEAD_DIM), cosine_table, sine_table))
    k_rot = low(rotate(k_norm.reshape(length, HEADS, HEAD_DIM), cosine_table, sine_table))
    attended = attention(q_rot, k_rot, v_proj.reshape(length, HEADS, HEAD_DIM))
    att_low = low(low_back(attended))
    branch_a = low_back(matmul_t(att_low, w_out))
    middle = inputs + branch_a * rms_scale(branch_a) * gain_table[:, 2]
    middle_low = low(middle)
    gate_proj = low_back(matmul(middle_low, w_gate))
    up_proj = low_back(matmul(middle_low, w_up))
    activated = low(jax.nn.silu(gate_proj) * up_proj)
    branch_f = low_back(matmul_t(activated, w_down))
    return middle + branch_f * rms_scale(branch_f) * gain_table[:, 3]

def reference(tokens, q_weight, k_weight, v_weight, o_weight, gate_weight, up_weight, down_weight, norm_gains, cotangent):
    weight_set = (q_weight.astype(jnp.float32), k_weight.astype(jnp.float32), v_weight.astype(jnp.float32), o_weight.astype(jnp.float32), gate_weight.astype(jnp.float32), up_weight.astype(jnp.float32), down_weight.astype(jnp.float32), norm_gains.astype(jnp.float32))

    def per_sequence(running, packed):
        seq_in, seq_cot = packed
        seq_out, pullback = jax.vjp(sequence_forward, seq_in, *weight_set)
        seq_grads = pullback(seq_cot)
        updated = tuple((total_now + grad_now for total_now, grad_now in zip(running, seq_grads[1:])))
        return (updated, (seq_out.astype(jnp.bfloat16), seq_grads[0]))
    initial = tuple((jnp.zeros_like(weight_now) for weight_now in weight_set))
    totals, (outputs, input_grads) = lax.scan(per_sequence, initial, (tokens.astype(jnp.float32), cotangent.astype(jnp.float32)))
    return (outputs, input_grads, totals[0], totals[1], totals[2], totals[3], totals[4], totals[5], totals[6], totals[7])
```

```python
import functools
import math

import jax
import jax.numpy as jnp
from jax import lax
from jax.experimental import pallas as pl
from jax.experimental.pallas import tpu as pltpu
from jax.sharding import PartitionSpec as P

HEAD_DIM = 128
LOG2E = 1.4426950408889634
ATTN_BLOCK = 512

norm_eps = 1e-06
rope_base = 500000.0
weight_axes = ("fsdp", "ctx")


def rms_scale(values_in):
    return lax.rsqrt(jnp.mean(values_in * values_in, axis=-1, keepdims=True) + norm_eps)


def rope_tables(length, offset):
    half_dim = HEAD_DIM // 2
    frequency = rope_base ** (-(jnp.arange(half_dim, dtype=jnp.float32) * 2.0) / HEAD_DIM)
    angles = (offset + jnp.arange(length, dtype=jnp.int32)).astype(jnp.float32)[
        :, None
    ] * frequency[None, :]
    return (jnp.cos(angles), jnp.sin(angles))


def rotate(values_in, cosine_table, sine_table):
    half_dim = values_in.shape[-1] // 2
    first_half = values_in[..., :half_dim]
    second_half = values_in[..., half_dim:]
    cosine = cosine_table[:, None, :]
    sine_part = sine_table[:, None, :]
    return jnp.concatenate(
        [
            first_half * cosine - second_half * sine_part,
            second_half * cosine + first_half * sine_part,
        ],
        axis=-1,
    )


def unrotate(grad_in, cosine_table, sine_table):
    return rotate(grad_in, cosine_table, -sine_table)


def dot_f32(left, right, left_dim, right_dim):
    return lax.dot_general(
        left,
        right,
        (((left_dim,), (right_dim,)), ((), ())),
        preferred_element_type=jnp.float32,
    )


def contract_rows(left, right):
    return dot_f32(left, right, 0, 0)


def contract_cols(left, right):
    return dot_f32(left, right, 1, 1)


def norm_backward(grad_in, values_in, scale_rows, gain_vec, dot_rows, model_width):
    cubed = scale_rows * scale_rows * scale_rows
    return scale_rows * (grad_in * gain_vec) - values_in * (cubed / model_width) * dot_rows


def causal(values_in, fill):
    keys = lax.broadcasted_iota(jnp.int32, values_in.shape, 0)
    queries = lax.broadcasted_iota(jnp.int32, values_in.shape, 1)
    return jnp.where(keys <= queries, values_in, fill)


def attn_fwd_kernel(q_ref, k_ref, v_ref, out_ref, lse_ref, max_s, sum_s, acc_s, *, block, scale):
    i = pl.program_id(1)
    q = q_ref[0]
    max_s[...] = jnp.full(max_s.shape, -1e30, jnp.float32)
    sum_s[...] = jnp.zeros_like(sum_s)
    acc_s[...] = jnp.zeros_like(acc_s)

    def step(j, diagonal):
        rows = pl.ds(pl.multiple_of(j * block, block), block)
        scores = dot_f32(k_ref[0, rows, :], q, 1, 1) * (scale * LOG2E)
        if diagonal:
            scores = causal(scores, -1e30)
        old_max = max_s[...]
        new_max = jnp.maximum(old_max, jnp.max(scores, axis=0, keepdims=True))
        decay = jnp.exp2(old_max - new_max)
        weights = jnp.exp2(scores - new_max)
        sum_s[...] = sum_s[...] * decay + jnp.sum(weights, axis=0, keepdims=True)
        max_s[...] = new_max
        acc_s[...] = acc_s[...] * decay + dot_f32(
            v_ref[0, rows, :], weights.astype(jnp.bfloat16), 0, 0
        )

    def body(j, carry):
        step(j, False)
        return carry

    lax.fori_loop(0, i, body, 0)
    step(i, True)
    total = sum_s[...]
    out_ref[0] = jnp.transpose(acc_s[...] / total).astype(jnp.bfloat16)
    lse_ref[0] = max_s[...] + jnp.log2(total)


def attn_fwd(packed):
    count, length, _ = packed.shape
    block = min(ATTN_BLOCK, length)
    rows = pl.BlockSpec((1, block, HEAD_DIM), lambda b, i: (b, i, 0))
    return pl.pallas_call(
        functools.partial(attn_fwd_kernel, block=block, scale=1.0 / math.sqrt(HEAD_DIM)),
        grid=(count, length // block),
        in_specs=[
            rows,
            pl.BlockSpec((1, length, HEAD_DIM), lambda b, i: (b, 0, 1)),
            pl.BlockSpec((1, length, HEAD_DIM), lambda b, i: (b, 0, 2)),
        ],
        out_specs=[rows, pl.BlockSpec((1, 1, block), lambda b, i: (b, 0, i))],
        out_shape=[
            jax.ShapeDtypeStruct((count, length, HEAD_DIM), jnp.bfloat16),
            jax.ShapeDtypeStruct((count, 1, length), jnp.float32),
        ],
        scratch_shapes=[
            pltpu.VMEM((1, block), jnp.float32),
            pltpu.VMEM((1, block), jnp.float32),
            pltpu.VMEM((HEAD_DIM, block), jnp.float32),
        ],
        cost_estimate=pl.CostEstimate(
            flops=2 * count * length * length * HEAD_DIM,
            bytes_accessed=10 * count * length * HEAD_DIM,
            transcendentals=count * length * length // 2,
        ),
        name="attn_fwd",
    )(packed, packed, packed)


def attn_bwd_kernel(
    q_ref, k_ref, v_ref, att_ref, grad_ref, lse_ref, out_ref, dk_s, dv_s, dq_s, *, block, scale, blocks
):
    i = pl.program_id(1)

    @pl.when(i == 0)
    def _():
        dk_s[...] = jnp.zeros_like(dk_s)
        dv_s[...] = jnp.zeros_like(dv_s)

    q = q_ref[0]
    grad = grad_ref[0]
    lse = lse_ref[0]
    delta = jnp.sum(
        jnp.transpose(grad.astype(jnp.float32) * att_ref[0].astype(jnp.float32)),
        axis=0,
        keepdims=True,
    )
    dq_s[...] = jnp.zeros_like(dq_s)

    def step(j, diagonal):
        rows = pl.ds(pl.multiple_of(j * block, block), block)
        k = k_ref[0, rows, :]
        probs = jnp.exp2(dot_f32(k, q, 1, 1) * (scale * LOG2E) - lse)
        if diagonal:
            probs = causal(probs, 0.0)
        dv_s[rows, :] += dot_f32(probs.astype(jnp.bfloat16), grad, 1, 0)
        d_probs = dot_f32(v_ref[0, rows, :], grad, 1, 1)
        d_scores = (probs * (d_probs - delta)).astype(jnp.bfloat16)
        dk_s[rows, :] += dot_f32(d_scores, q, 1, 0)
        dq_s[...] += dot_f32(k, d_scores, 0, 0)

    def body(j, carry):
        step(j, False)
        return carry

    lax.fori_loop(0, i, body, 0)
    step(i, True)
    here = pl.ds(pl.multiple_of(i * block, block), block)
    out_ref[0, here, 0:HEAD_DIM] = (jnp.transpose(dq_s[...]) * scale).astype(jnp.bfloat16)

    @pl.when(i == blocks - 1)
    def _():
        out_ref[0, :, HEAD_DIM : 2 * HEAD_DIM] = (dk_s[...] * scale).astype(jnp.bfloat16)
        out_ref[0, :, 2 * HEAD_DIM : 3 * HEAD_DIM] = dv_s[...].astype(jnp.bfloat16)


def attn_bwd(packed, attended, grad, lse):
    count, length, _ = packed.shape
    block = min(ATTN_BLOCK, length)
    rows = pl.BlockSpec((1, block, HEAD_DIM), lambda b, i: (b, i, 0))
    return pl.pallas_call(
        functools.partial(
            attn_bwd_kernel,
            block=block,
            scale=1.0 / math.sqrt(HEAD_DIM),
            blocks=length // block,
        ),
        grid=(count, length // block),
        in_specs=[
            rows,
            pl.BlockSpec((1, length, HEAD_DIM), lambda b, i: (b, 0, 1)),
            pl.BlockSpec((1, length, HEAD_DIM), lambda b, i: (b, 0, 2)),
            rows,
            rows,
            pl.BlockSpec((1, 1, block), lambda b, i: (b, 0, i)),
        ],
        out_specs=pl.BlockSpec((1, length, 3 * HEAD_DIM), lambda b, i: (b, 0, 0)),
        out_shape=jax.ShapeDtypeStruct((count, length, 3 * HEAD_DIM), jnp.bfloat16),
        scratch_shapes=[
            pltpu.VMEM((length, HEAD_DIM), jnp.float32),
            pltpu.VMEM((length, HEAD_DIM), jnp.float32),
            pltpu.VMEM((HEAD_DIM, block), jnp.float32),
        ],
        cost_estimate=pl.CostEstimate(
            flops=5 * count * length * length * HEAD_DIM,
            bytes_accessed=18 * count * length * HEAD_DIM,
            transcendentals=count * length * length // 2,
        ),
        name="attn_bwd",
    )(packed, packed, packed, attended, grad, lse)


def to_heads(values_in, ctx_size):
    seqs, span, heads, width = values_in.shape
    each = heads // ctx_size
    parts = values_in.reshape(seqs, span, ctx_size, each, width).transpose(2, 0, 3, 1, 4)
    parts = lax.all_to_all(parts, "ctx", 0, 0, tiled=True)
    return parts.transpose(1, 2, 0, 3, 4).reshape(seqs * each, ctx_size * span, width)


def to_positions(values_in, seqs, ctx_size):
    count, length, width = values_in.shape
    each, span = count // seqs, length // ctx_size
    parts = values_in.reshape(seqs, each, ctx_size, span, width).transpose(2, 0, 1, 3, 4)
    parts = lax.all_to_all(parts, "ctx", 0, 0, tiled=True)
    return parts.transpose(1, 3, 0, 2, 4).reshape(seqs, span, ctx_size * each, width)


def tensor_sum(values_in):
    return lax.psum(values_in.astype(jnp.bfloat16), "tp").astype(jnp.float32)


def gather_rows(values_in):
    return lax.all_gather(values_in, weight_axes, axis=0, tiled=True)


def scatter_rows(values_in):
    return lax.psum_scatter(
        values_in.astype(jnp.bfloat16), weight_axes, scatter_dimension=0, tiled=True
    ).astype(jnp.float32)


def per_device(
    tokens,
    q_weight,
    k_weight,
    v_weight,
    o_weight,
    gate_weight,
    up_weight,
    down_weight,
    norm_gains,
    cotangent,
):
    seq_count, seq_span, model_width = tokens.shape
    row_count = seq_count * seq_span
    tensor = lax.axis_size("tp")
    ctx_size = lax.axis_size("ctx")
    local_width = model_width // tensor
    hidden = gate_weight.shape[1]
    heads_here = local_width // HEAD_DIM
    feature_start = lax.axis_index("tp") * local_width
    position = lax.axis_index("ctx") * seq_span
    q_shape = (seq_count, seq_span, heads_here, HEAD_DIM)

    w_qkv = gather_rows(jnp.concatenate([q_weight, k_weight, v_weight], axis=1))
    w_out = gather_rows(o_weight)
    w_gate_up = gather_rows(jnp.concatenate([gate_weight, up_weight], axis=1))
    w_down = gather_rows(down_weight)
    gain_table = gather_rows(norm_gains).astype(jnp.float32)
    gain_q = lax.dynamic_slice_in_dim(gain_table[:, 0], feature_start, local_width)
    gain_k = lax.dynamic_slice_in_dim(gain_table[:, 1], feature_start, local_width)
    gain_attn = gain_table[:, 2]
    gain_ffn = gain_table[:, 3]
    inputs = tokens.reshape(row_count, model_width)
    cosine_table, sine_table = rope_tables(seq_span, position)

    qkv_proj = jnp.dot(inputs, w_qkv, preferred_element_type=jnp.float32)
    q_proj = qkv_proj[:, :local_width]
    k_proj = qkv_proj[:, local_width : 2 * local_width]
    v_low = qkv_proj[:, 2 * local_width :].astype(jnp.bfloat16)
    q_squares, k_squares = lax.psum(
        (jnp.sum(q_proj * q_proj, axis=1), jnp.sum(k_proj * k_proj, axis=1)), "tp"
    )
    q_rs = lax.rsqrt(q_squares / model_width + norm_eps)[:, None]
    k_rs = lax.rsqrt(k_squares / model_width + norm_eps)[:, None]
    q_rot = rotate((q_proj * q_rs * gain_q).reshape(q_shape), cosine_table, sine_table)
    k_rot = rotate((k_proj * k_rs * gain_k).reshape(q_shape), cosine_table, sine_table)
    packed = to_heads(
        jnp.concatenate(
            [q_rot.astype(jnp.bfloat16), k_rot.astype(jnp.bfloat16), v_low.reshape(q_shape)], axis=-1
        ),
        ctx_size,
    )
    attended, log_total = attn_fwd(packed)
    att_low = to_positions(attended, seq_count, ctx_size).reshape(row_count, local_width)
    branch_a = tensor_sum(contract_cols(att_low, w_out))
    a_rs = rms_scale(branch_a)
    middle = inputs.astype(jnp.float32) + branch_a * a_rs * gain_attn
    middle_low = middle.astype(jnp.bfloat16)
    gate_up = jnp.dot(middle_low, w_gate_up, preferred_element_type=jnp.float32)
    gate_proj = gate_up[:, :hidden]
    up_proj = gate_up[:, hidden:]
    activated = (jax.nn.silu(gate_proj) * up_proj).astype(jnp.bfloat16)
    branch_f = tensor_sum(contract_cols(activated, w_down))
    f_rs = rms_scale(branch_f)
    block_out = (
        (middle + branch_f * f_rs * gain_ffn)
        .astype(jnp.bfloat16)
        .reshape(seq_count, seq_span, model_width)
    )
    grad_out = cotangent.reshape(row_count, model_width).astype(jnp.float32)
    ffn_gain_part = jnp.sum(grad_out * branch_f * f_rs, axis=0)
    ffn_dot = jnp.sum(grad_out * gain_ffn * branch_f, axis=1, keepdims=True)
    d_branch_f = norm_backward(grad_out, branch_f, f_rs, gain_ffn, ffn_dot, model_width).astype(
        jnp.bfloat16
    )
    down_grad = scatter_rows(contract_rows(d_branch_f, activated))
    d_act = jnp.dot(d_branch_f, w_down, preferred_element_type=jnp.float32)
    sigmoid_gate = jax.nn.sigmoid(gate_proj)
    d_gate = (d_act * up_proj * sigmoid_gate * (1.0 + gate_proj * (1.0 - sigmoid_gate))).astype(
        jnp.bfloat16
    )
    d_up = (d_act * gate_proj * sigmoid_gate).astype(jnp.bfloat16)
    d_gate_up = jnp.concatenate([d_gate, d_up], axis=1)
    d_middle = grad_out + tensor_sum(contract_cols(d_gate_up, w_gate_up))
    gate_up_grad = scatter_rows(contract_rows(middle_low, d_gate_up))
    attn_gain_part = jnp.sum(d_middle * branch_a * a_rs, axis=0)
    attn_dot = jnp.sum(d_middle * gain_attn * branch_a, axis=1, keepdims=True)
    d_branch_a = norm_backward(d_middle, branch_a, a_rs, gain_attn, attn_dot, model_width).astype(
        jnp.bfloat16
    )
    d_att = jnp.dot(d_branch_a, w_out, preferred_element_type=jnp.float32).astype(jnp.bfloat16)
    out_grad = scatter_rows(contract_rows(d_branch_a, att_low))
    d_packed = to_positions(
        attn_bwd(packed, attended, to_heads(d_att.reshape(q_shape), ctx_size), log_total),
        seq_count,
        ctx_size,
    )
    d_q_rot = d_packed[..., :HEAD_DIM].astype(jnp.float32)
    d_k_rot = d_packed[..., HEAD_DIM : 2 * HEAD_DIM].astype(jnp.float32)
    d_value = d_packed[..., 2 * HEAD_DIM :].reshape(row_count, local_width)
    d_q_norm = unrotate(d_q_rot, cosine_table, sine_table).reshape(row_count, local_width)
    d_k_norm = unrotate(d_k_rot, cosine_table, sine_table).reshape(row_count, local_width)
    query_gain_part = jnp.sum(d_q_norm * q_proj * q_rs, axis=0)
    key_gain_part = jnp.sum(d_k_norm * k_proj * k_rs, axis=0)
    pre_gains = lax.dynamic_update_slice(
        jnp.zeros((model_width, 2), jnp.float32),
        jnp.stack([query_gain_part, key_gain_part], axis=1),
        (feature_start, 0),
    )
    is_first = lax.axis_index("tp") == 0
    post_gains = jnp.where(is_first, jnp.stack([attn_gain_part, ffn_gain_part], axis=1), 0.0)
    gain_part = jnp.concatenate([pre_gains, post_gains], axis=1)
    query_dot, key_dot, gain_sum = lax.psum(
        (
            jnp.sum(d_q_norm * gain_q * q_proj, axis=1),
            jnp.sum(d_k_norm * gain_k * k_proj, axis=1),
            gain_part,
        ),
        "tp",
    )
    d_query = norm_backward(d_q_norm, q_proj, q_rs, gain_q, query_dot[:, None], model_width)
    d_key = norm_backward(d_k_norm, k_proj, k_rs, gain_k, key_dot[:, None], model_width)
    d_qkv = jnp.concatenate(
        [d_query.astype(jnp.bfloat16), d_key.astype(jnp.bfloat16), d_value], axis=1
    )
    token_grad = (d_middle + tensor_sum(contract_cols(d_qkv, w_qkv))).reshape(
        seq_count, seq_span, model_width
    )
    qkv_grad = scatter_rows(contract_rows(inputs, d_qkv))
    gain_grad = lax.psum_scatter(gain_sum, weight_axes, scatter_dimension=0, tiled=True)
    return (
        block_out,
        token_grad,
        qkv_grad[:, :local_width],
        qkv_grad[:, local_width : 2 * local_width],
        qkv_grad[:, 2 * local_width :],
        out_grad,
        gate_up_grad[:, :hidden],
        gate_up_grad[:, hidden:],
        down_grad,
        gain_grad,
    )


def solution(mesh):
    weight_spec = P(weight_axes, "tp")
    token_spec = P("fsdp", "ctx", None)
    return jax.shard_map(
        per_device,
        mesh=mesh,
        in_specs=(token_spec,) + (weight_spec,) * 7 + (P(weight_axes, None), token_spec),
        out_specs=(token_spec, token_spec) + (weight_spec,) * 7 + (P(weight_axes, None),),
        check_vma=False,
    )
```

```python
import functools
import math

import jax
import jax.numpy as jnp
from jax import lax
from jax.experimental import pallas as pl
from jax.experimental.pallas import tpu as pltpu
from jax.sharding import PartitionSpec as P


HEAD_DIM = 128
LOG2E = 1.4426950408889634
ATTN_BLOCK = 512

norm_eps = 1e-06
rope_base = 500000.0
weight_axes = ("fsdp", "ctx")


def rms_scale(values_in):
    return lax.rsqrt(jnp.mean(values_in * values_in, axis=-1, keepdims=True) + norm_eps)


def rope_tables(length, offset):
    half_dim = HEAD_DIM // 2
    frequency = rope_base ** (-(jnp.arange(half_dim, dtype=jnp.float32) * 2.0) / HEAD_DIM)
    angles = (offset + jnp.arange(length, dtype=jnp.int32)).astype(jnp.float32)[
        :, None
    ] * frequency[None, :]
    return (jnp.cos(angles), jnp.sin(angles))


def rotate(values_in, cosine_table, sine_table):
    half_dim = values_in.shape[-1] // 2
    first_half = values_in[..., :half_dim]
    second_half = values_in[..., half_dim:]
    cosine = cosine_table[:, None, :]
    sine_part = sine_table[:, None, :]
    return jnp.concatenate(
        [
            first_half * cosine - second_half * sine_part,
            second_half * cosine + first_half * sine_part,
        ],
        axis=-1,
    )


def unrotate(grad_in, cosine_table, sine_table):
    return rotate(grad_in, cosine_table, -sine_table)


def dot_f32(left, right, left_dim, right_dim):
    return lax.dot_general(
        left,
        right,
        (((left_dim,), (right_dim,)), ((), ())),
        preferred_element_type=jnp.float32,
    )


def contract_rows(left, right):
    return dot_f32(left, right, 0, 0)


def contract_cols(left, right):
    return dot_f32(left, right, 1, 1)


def norm_backward(grad_in, values_in, scale_rows, gain_vec, dot_rows, model_width):
    cubed = scale_rows * scale_rows * scale_rows
    return scale_rows * (grad_in * gain_vec) - values_in * (cubed / model_width) * dot_rows


def causal(values_in, fill):
    keys = lax.broadcasted_iota(jnp.int32, values_in.shape, 0)
    queries = lax.broadcasted_iota(jnp.int32, values_in.shape, 1)
    return jnp.where(keys <= queries, values_in, fill)


def attn_fwd_kernel(q_ref, k_ref, v_ref, out_ref, lse_ref, max_s, sum_s, acc_s, *, block, scale):
    i = pl.program_id(1)
    q = q_ref[0]
    max_s[...] = jnp.full(max_s.shape, -1e30, jnp.float32)
    sum_s[...] = jnp.zeros_like(sum_s)
    acc_s[...] = jnp.zeros_like(acc_s)

    def step(j, diagonal):
        rows = pl.ds(pl.multiple_of(j * block, block), block)
        scores = dot_f32(k_ref[0, rows, :], q, 1, 1) * (scale * LOG2E)
        if diagonal:
            scores = causal(scores, -1e30)
        old_max = max_s[...]
        new_max = jnp.maximum(old_max, jnp.max(scores, axis=0, keepdims=True))
        decay = jnp.exp2(old_max - new_max)
        weights = jnp.exp2(scores - new_max)
        sum_s[...] = sum_s[...] * decay + jnp.sum(weights, axis=0, keepdims=True)
        max_s[...] = new_max
        acc_s[...] = acc_s[...] * decay + dot_f32(
            v_ref[0, rows, :], weights.astype(jnp.bfloat16), 0, 0
        )

    def body(j, carry):
        step(j, False)
        return carry

    lax.fori_loop(0, i, body, 0)
    step(i, True)
    total = sum_s[...]
    out_ref[0] = jnp.transpose(acc_s[...] / total).astype(jnp.bfloat16)
    lse_ref[0] = max_s[...] + jnp.log2(total)


def attn_fwd(packed):
    count, length, _ = packed.shape
    block = min(ATTN_BLOCK, length)
    rows = pl.BlockSpec((1, block, HEAD_DIM), lambda b, i: (b, i, 0))
    return pl.pallas_call(
        functools.partial(attn_fwd_kernel, block=block, scale=1.0 / math.sqrt(HEAD_DIM)),
        grid=(count, length // block),
        in_specs=[
            rows,
            pl.BlockSpec((1, length, HEAD_DIM), lambda b, i: (b, 0, 1)),
            pl.BlockSpec((1, length, HEAD_DIM), lambda b, i: (b, 0, 2)),
        ],
        out_specs=[rows, pl.BlockSpec((1, 1, block), lambda b, i: (b, 0, i))],
        out_shape=[
            jax.ShapeDtypeStruct((count, length, HEAD_DIM), jnp.bfloat16),
            jax.ShapeDtypeStruct((count, 1, length), jnp.float32),
        ],
        scratch_shapes=[
            pltpu.VMEM((1, block), jnp.float32),
            pltpu.VMEM((1, block), jnp.float32),
            pltpu.VMEM((HEAD_DIM, block), jnp.float32),
        ],
        cost_estimate=pl.CostEstimate(
            flops=2 * count * length * length * HEAD_DIM,
            bytes_accessed=10 * count * length * HEAD_DIM,
            transcendentals=count * length * length // 2,
        ),
        name="attn_fwd",
    )(packed, packed, packed)


def attn_bwd_kernel(
    q_ref, k_ref, v_ref, att_ref, grad_ref, lse_ref, out_ref, dk_s, dv_s, dq_s, *, block, scale, blocks
):
    i = pl.program_id(1)

    @pl.when(i == 0)
    def _():
        dk_s[...] = jnp.zeros_like(dk_s)
        dv_s[...] = jnp.zeros_like(dv_s)

    q = q_ref[0]
    grad = grad_ref[0]
    lse = lse_ref[0]
    delta = jnp.sum(
        jnp.transpose(grad.astype(jnp.float32) * att_ref[0].astype(jnp.float32)),
        axis=0,
        keepdims=True,
    )
    dq_s[...] = jnp.zeros_like(dq_s)

    def step(j, diagonal):
        rows = pl.ds(pl.multiple_of(j * block, block), block)
        k = k_ref[0, rows, :]
        probs = jnp.exp2(dot_f32(k, q, 1, 1) * (scale * LOG2E) - lse)
        if diagonal:
            probs = causal(probs, 0.0)
        dv_s[rows, :] += dot_f32(probs.astype(jnp.bfloat16), grad, 1, 0)
        d_probs = dot_f32(v_ref[0, rows, :], grad, 1, 1)
        d_scores = (probs * (d_probs - delta)).astype(jnp.bfloat16)
        dk_s[rows, :] += dot_f32(d_scores, q, 1, 0)
        dq_s[...] += dot_f32(k, d_scores, 0, 0)

    def body(j, carry):
        step(j, False)
        return carry

    lax.fori_loop(0, i, body, 0)
    step(i, True)
    here = pl.ds(pl.multiple_of(i * block, block), block)
    out_ref[0, here, 0:HEAD_DIM] = (jnp.transpose(dq_s[...]) * scale).astype(jnp.bfloat16)

    @pl.when(i == blocks - 1)
    def _():
        out_ref[0, :, HEAD_DIM : 2 * HEAD_DIM] = (dk_s[...] * scale).astype(jnp.bfloat16)
        out_ref[0, :, 2 * HEAD_DIM : 3 * HEAD_DIM] = dv_s[...].astype(jnp.bfloat16)


def attn_bwd(packed, attended, grad, lse):
    count, length, _ = packed.shape
    block = min(ATTN_BLOCK, length)
    rows = pl.BlockSpec((1, block, HEAD_DIM), lambda b, i: (b, i, 0))
    return pl.pallas_call(
        functools.partial(
            attn_bwd_kernel,
            block=block,
            scale=1.0 / math.sqrt(HEAD_DIM),
            blocks=length // block,
        ),
        grid=(count, length // block),
        in_specs=[
            rows,
            pl.BlockSpec((1, length, HEAD_DIM), lambda b, i: (b, 0, 1)),
            pl.BlockSpec((1, length, HEAD_DIM), lambda b, i: (b, 0, 2)),
            rows,
            rows,
            pl.BlockSpec((1, 1, block), lambda b, i: (b, 0, i)),
        ],
        out_specs=pl.BlockSpec((1, length, 3 * HEAD_DIM), lambda b, i: (b, 0, 0)),
        out_shape=jax.ShapeDtypeStruct((count, length, 3 * HEAD_DIM), jnp.bfloat16),
        scratch_shapes=[
            pltpu.VMEM((length, HEAD_DIM), jnp.float32),
            pltpu.VMEM((length, HEAD_DIM), jnp.float32),
            pltpu.VMEM((HEAD_DIM, block), jnp.float32),
        ],
        cost_estimate=pl.CostEstimate(
            flops=5 * count * length * length * HEAD_DIM,
            bytes_accessed=18 * count * length * HEAD_DIM,
            transcendentals=count * length * length // 2,
        ),
        name="attn_bwd",
    )(packed, packed, packed, attended, grad, lse)


def to_heads(values_in, ctx_size):
    seqs, span, heads, width = values_in.shape
    each = heads // ctx_size
    parts = values_in.reshape(seqs, span, ctx_size, each, width).transpose(2, 0, 3, 1, 4)
    parts = lax.all_to_all(parts, "ctx", 0, 0, tiled=True)
    return parts.transpose(1, 2, 0, 3, 4).reshape(seqs * each, ctx_size * span, width)


def to_positions(values_in, seqs, ctx_size):
    count, length, width = values_in.shape
    each, span = count // seqs, length // ctx_size
    parts = values_in.reshape(seqs, each, ctx_size, span, width).transpose(2, 0, 1, 3, 4)
    parts = lax.all_to_all(parts, "ctx", 0, 0, tiled=True)
    return parts.transpose(1, 3, 0, 2, 4).reshape(seqs, span, ctx_size * each, width)


def tensor_sum(values_in):
    values_in = values_in.astype(jnp.bfloat16)
    total = lax.psum(values_in, "tp")
    return total.astype(jnp.float32)


def gather_rows(values_in):
    return lax.all_gather(values_in, weight_axes, axis=0, tiled=True)


def scatter_rows(values_in):
    values_in = values_in.astype(jnp.bfloat16)
    return lax.psum_scatter(values_in, weight_axes, scatter_dimension=0, tiled=True)


def per_device(
    tokens,
    q_weight,
    k_weight,
    v_weight,
    o_weight,
    gate_weight,
    up_weight,
    down_weight,
    norm_gains,
    cotangent,
):
    seq_count, seq_span, model_width = tokens.shape
    row_count = seq_count * seq_span
    tensor = lax.axis_size("tp")
    ctx_size = lax.axis_size("ctx")
    local_width = model_width // tensor
    hidden = gate_weight.shape[1]
    heads_here = local_width // HEAD_DIM
    feature_start = lax.axis_index("tp") * local_width
    position = lax.axis_index("ctx") * seq_span
    q_shape = (seq_count, seq_span, heads_here, HEAD_DIM)

    w_qkv = gather_rows(jnp.concatenate([q_weight, k_weight, v_weight], axis=1))
    w_out = gather_rows(o_weight)
    w_gate_up = gather_rows(jnp.concatenate([gate_weight, up_weight], axis=1))
    w_down = gather_rows(down_weight)
    gain_table = gather_rows(norm_gains).astype(jnp.float32)
    gain_q = lax.dynamic_slice_in_dim(gain_table[:, 0], feature_start, local_width)
    gain_k = lax.dynamic_slice_in_dim(gain_table[:, 1], feature_start, local_width)
    gain_attn = gain_table[:, 2]
    gain_ffn = gain_table[:, 3]
    inputs = tokens.reshape(row_count, model_width)
    cosine_table, sine_table = rope_tables(seq_span, position)

    qkv_proj = jnp.dot(inputs, w_qkv, preferred_element_type=jnp.float32)
    q_proj = qkv_proj[:, :local_width]
    k_proj = qkv_proj[:, local_width : 2 * local_width]
    v_low = qkv_proj[:, 2 * local_width :].astype(jnp.bfloat16)
    q_squares, k_squares = lax.psum(
        (jnp.sum(q_proj * q_proj, axis=1), jnp.sum(k_proj * k_proj, axis=1)), "tp"
    )
    q_rs = lax.rsqrt(q_squares / model_width + norm_eps)[:, None]
    k_rs = lax.rsqrt(k_squares / model_width + norm_eps)[:, None]
    q_rot = rotate((q_proj * q_rs * gain_q).reshape(q_shape), cosine_table, sine_table)
    k_rot = rotate((k_proj * k_rs * gain_k).reshape(q_shape), cosine_table, sine_table)
    packed = to_heads(
        jnp.concatenate(
            [q_rot.astype(jnp.bfloat16), k_rot.astype(jnp.bfloat16), v_low.reshape(q_shape)], axis=-1
        ),
        ctx_size,
    )
    attended, log_total = attn_fwd(packed)
    att_low = to_positions(attended, seq_count, ctx_size).reshape(row_count, local_width)
    branch_a = tensor_sum(contract_cols(att_low, w_out))
    a_rs = rms_scale(branch_a)
    middle = inputs.astype(jnp.float32) + branch_a * a_rs * gain_attn
    middle_low = middle.astype(jnp.bfloat16)
    gate_up = jnp.dot(middle_low, w_gate_up, preferred_element_type=jnp.float32)
    gate_proj = gate_up[:, :hidden]
    up_proj = gate_up[:, hidden:]
    activated = (jax.nn.silu(gate_proj) * up_proj).astype(jnp.bfloat16)
    branch_f = tensor_sum(contract_cols(activated, w_down))
    f_rs = rms_scale(branch_f)
    block_out = (
        (middle + branch_f * f_rs * gain_ffn)
        .astype(jnp.bfloat16)
        .reshape(seq_count, seq_span, model_width)
    )
    grad_out = cotangent.reshape(row_count, model_width).astype(jnp.float32)
    ffn_gain_part = jnp.sum(grad_out * branch_f * f_rs, axis=0)
    ffn_dot = jnp.sum(grad_out * gain_ffn * branch_f, axis=1, keepdims=True)
    d_branch_f = norm_backward(grad_out, branch_f, f_rs, gain_ffn, ffn_dot, model_width).astype(
        jnp.bfloat16
    )
    down_part = contract_rows(d_branch_f, activated)
    down_grad = scatter_rows(down_part).astype(jnp.float32)
    d_act = jnp.dot(d_branch_f, w_down, preferred_element_type=jnp.float32)
    sigmoid_gate = jax.nn.sigmoid(gate_proj)
    d_gate = (d_act * up_proj * sigmoid_gate * (1.0 + gate_proj * (1.0 - sigmoid_gate))).astype(
        jnp.bfloat16
    )
    d_up = (d_act * gate_proj * sigmoid_gate).astype(jnp.bfloat16)
    d_gate_up = jnp.concatenate([d_gate, d_up], axis=1)
    d_middle = grad_out + tensor_sum(contract_cols(d_gate_up, w_gate_up))
    gate_up_part = contract_rows(middle_low, d_gate_up)
    gate_up_grad = scatter_rows(gate_up_part).astype(jnp.float32)
    attn_gain_part = jnp.sum(d_middle * branch_a * a_rs, axis=0)
    attn_dot = jnp.sum(d_middle * gain_attn * branch_a, axis=1, keepdims=True)
    d_branch_a = norm_backward(d_middle, branch_a, a_rs, gain_attn, attn_dot, model_width).astype(
        jnp.bfloat16
    )
    d_att = jnp.dot(d_branch_a, w_out, preferred_element_type=jnp.float32).astype(jnp.bfloat16)
    out_part = contract_rows(d_branch_a, att_low)
    out_grad = scatter_rows(out_part).astype(jnp.float32)
    d_packed = to_positions(
        attn_bwd(packed, attended, to_heads(d_att.reshape(q_shape), ctx_size), log_total),
        seq_count,
        ctx_size,
    )
    d_q_rot = d_packed[..., :HEAD_DIM].astype(jnp.float32)
    d_k_rot = d_packed[..., HEAD_DIM : 2 * HEAD_DIM].astype(jnp.float32)
    d_value = d_packed[..., 2 * HEAD_DIM :].reshape(row_count, local_width)
    d_q_norm = unrotate(d_q_rot, cosine_table, sine_table).reshape(row_count, local_width)
    d_k_norm = unrotate(d_k_rot, cosine_table, sine_table).reshape(row_count, local_width)
    query_gain_part = jnp.sum(d_q_norm * q_proj * q_rs, axis=0)
    key_gain_part = jnp.sum(d_k_norm * k_proj * k_rs, axis=0)
    pre_gains = lax.dynamic_update_slice(
        jnp.zeros((2, model_width), jnp.float32),
        jnp.stack([query_gain_part, key_gain_part]),
        (0, feature_start),
    )
    is_first = lax.axis_index("tp") == 0
    post_gains = jnp.where(is_first, jnp.stack([attn_gain_part, ffn_gain_part]), 0.0)
    query_dot, key_dot, gain_sum = lax.psum(
        (
            jnp.sum(d_q_norm * gain_q * q_proj, axis=1),
            jnp.sum(d_k_norm * gain_k * k_proj, axis=1),
            jnp.concatenate([pre_gains, post_gains], axis=0),
        ),
        "tp",
    )
    gain_high = gain_sum.astype(jnp.bfloat16)
    gain_rest = (gain_sum - gain_high.astype(jnp.float32)).astype(jnp.bfloat16)
    gain_terms = jnp.concatenate([gain_high, gain_rest], axis=0).T
    gain_terms = jnp.pad(gain_terms, ((0, 0), (0, HEAD_DIM - gain_terms.shape[1])))
    d_query = norm_backward(d_q_norm, q_proj, q_rs, gain_q, query_dot[:, None], model_width)
    d_key = norm_backward(d_k_norm, k_proj, k_rs, gain_k, key_dot[:, None], model_width)
    d_qkv = jnp.concatenate(
        [d_query.astype(jnp.bfloat16), d_key.astype(jnp.bfloat16), d_value], axis=1
    )
    token_grad = (d_middle + tensor_sum(contract_cols(d_qkv, w_qkv))).reshape(
        seq_count, seq_span, model_width
    )
    qkv_part = contract_rows(inputs, d_qkv).astype(jnp.bfloat16)
    last_grad = scatter_rows(jnp.concatenate([qkv_part, gain_terms], axis=1)).astype(jnp.float32)
    qkv_grad = last_grad[:, : 3 * local_width]
    gain_grad = (
        last_grad[:, 3 * local_width : 3 * local_width + 4]
        + last_grad[:, 3 * local_width + 4 : 3 * local_width + 8]
    )
    return (
        block_out,
        token_grad,
        qkv_grad[:, :local_width],
        qkv_grad[:, local_width : 2 * local_width],
        qkv_grad[:, 2 * local_width :],
        out_grad,
        gate_up_grad[:, :hidden],
        gate_up_grad[:, hidden:],
        down_grad,
        gain_grad,
    )


def solution(mesh):
    weight_spec = P(weight_axes, "tp")
    token_spec = P("fsdp", "ctx", None)
    return jax.shard_map(
        per_device,
        mesh=mesh,
        in_specs=(token_spec,) + (weight_spec,) * 7 + (P(weight_axes, None), token_spec),
        out_specs=(token_spec, token_spec) + (weight_spec,) * 7 + (P(weight_axes, None),),
        check_vma=False,
    )
```

```python
import functools
import math

import jax
import jax.numpy as jnp
from jax import lax
from jax.experimental import pallas as pl
from jax.experimental.pallas import tpu as pltpu
from jax.sharding import PartitionSpec as P


HEAD_DIM = 128
LOG2E = 1.4426950408889634
ATTN_BLOCK = 512

norm_eps = 1e-06
rope_base = 500000.0
weight_axes = ("fsdp", "ctx")


def rms_scale(values_in):
    return lax.rsqrt(jnp.mean(values_in * values_in, axis=-1, keepdims=True) + norm_eps)


def rope_tables(length, offset):
    half_dim = HEAD_DIM // 2
    frequency = rope_base ** (-(jnp.arange(half_dim, dtype=jnp.float32) * 2.0) / HEAD_DIM)
    angles = (offset + jnp.arange(length, dtype=jnp.int32)).astype(jnp.float32)[
        :, None
    ] * frequency[None, :]
    return (jnp.cos(angles), jnp.sin(angles))


def rotate(values_in, cosine_table, sine_table):
    half_dim = values_in.shape[-1] // 2
    first_half = values_in[..., :half_dim]
    second_half = values_in[..., half_dim:]
    cosine = cosine_table[:, None, :]
    sine_part = sine_table[:, None, :]
    return jnp.concatenate(
        [
            first_half * cosine - second_half * sine_part,
            second_half * cosine + first_half * sine_part,
        ],
        axis=-1,
    )


def unrotate(grad_in, cosine_table, sine_table):
    return rotate(grad_in, cosine_table, -sine_table)


def dot_f32(left, right, left_dim, right_dim):
    return lax.dot_general(
        left,
        right,
        (((left_dim,), (right_dim,)), ((), ())),
        preferred_element_type=jnp.float32,
    )


def contract_rows(left, right):
    return dot_f32(left, right, 0, 0)


def contract_cols(left, right):
    return dot_f32(left, right, 1, 1)


def norm_backward(grad_in, values_in, scale_rows, gain_vec, dot_rows, model_width):
    cubed = scale_rows * scale_rows * scale_rows
    return scale_rows * (grad_in * gain_vec) - values_in * (cubed / model_width) * dot_rows


def causal(values_in, fill):
    keys = lax.broadcasted_iota(jnp.int32, values_in.shape, 0)
    queries = lax.broadcasted_iota(jnp.int32, values_in.shape, 1)
    return jnp.where(keys <= queries, values_in, fill)


def attn_fwd_kernel(q_ref, k_ref, v_ref, out_ref, lse_ref, max_s, sum_s, acc_s, *, block, scale):
    i = pl.program_id(1)
    q = q_ref[0]
    max_s[...] = jnp.full(max_s.shape, -1e30, jnp.float32)
    sum_s[...] = jnp.zeros_like(sum_s)
    acc_s[...] = jnp.zeros_like(acc_s)

    def step(j, diagonal):
        rows = pl.ds(pl.multiple_of(j * block, block), block)
        scores = dot_f32(k_ref[0, rows, :], q, 1, 1) * (scale * LOG2E)
        if diagonal:
            scores = causal(scores, -1e30)
        old_max = max_s[...]
        new_max = jnp.maximum(old_max, jnp.max(scores, axis=0, keepdims=True))
        decay = jnp.exp2(old_max - new_max)
        weights = jnp.exp2(scores - new_max)
        sum_s[...] = sum_s[...] * decay + jnp.sum(weights, axis=0, keepdims=True)
        max_s[...] = new_max
        acc_s[...] = acc_s[...] * decay + dot_f32(
            v_ref[0, rows, :], weights.astype(jnp.bfloat16), 0, 0
        )

    def body(j, carry):
        step(j, False)
        return carry

    lax.fori_loop(0, i, body, 0)
    step(i, True)
    total = sum_s[...]
    out_ref[0] = jnp.transpose(acc_s[...] / total).astype(jnp.bfloat16)
    lse_ref[0] = max_s[...] + jnp.log2(total)


def attn_fwd(packed):
    count, length, _ = packed.shape
    block = min(ATTN_BLOCK, length)
    rows = pl.BlockSpec((1, block, HEAD_DIM), lambda b, i: (b, i, 0))
    return pl.pallas_call(
        functools.partial(attn_fwd_kernel, block=block, scale=1.0 / math.sqrt(HEAD_DIM)),
        grid=(count, length // block),
        in_specs=[
            rows,
            pl.BlockSpec((1, length, HEAD_DIM), lambda b, i: (b, 0, 1)),
            pl.BlockSpec((1, length, HEAD_DIM), lambda b, i: (b, 0, 2)),
        ],
        out_specs=[rows, pl.BlockSpec((1, 1, block), lambda b, i: (b, 0, i))],
        out_shape=[
            jax.ShapeDtypeStruct((count, length, HEAD_DIM), jnp.bfloat16),
            jax.ShapeDtypeStruct((count, 1, length), jnp.float32),
        ],
        scratch_shapes=[
            pltpu.VMEM((1, block), jnp.float32),
            pltpu.VMEM((1, block), jnp.float32),
            pltpu.VMEM((HEAD_DIM, block), jnp.float32),
        ],
        cost_estimate=pl.CostEstimate(
            flops=2 * count * length * length * HEAD_DIM,
            bytes_accessed=10 * count * length * HEAD_DIM,
            transcendentals=count * length * length // 2,
        ),
        name="attn_fwd",
    )(packed, packed, packed)


def attn_bwd_kernel(
    q_ref, k_ref, v_ref, att_ref, grad_ref, lse_ref, out_ref, dk_s, dv_s, dq_s, *, block, scale, blocks
):
    i = pl.program_id(1)

    @pl.when(i == 0)
    def _():
        dk_s[...] = jnp.zeros_like(dk_s)
        dv_s[...] = jnp.zeros_like(dv_s)

    q = q_ref[0]
    grad = grad_ref[0]
    lse = lse_ref[0]
    delta = jnp.sum(
        jnp.transpose(grad.astype(jnp.float32) * att_ref[0].astype(jnp.float32)),
        axis=0,
        keepdims=True,
    )
    dq_s[...] = jnp.zeros_like(dq_s)

    def step(j, diagonal):
        rows = pl.ds(pl.multiple_of(j * block, block), block)
        k = k_ref[0, rows, :]
        probs = jnp.exp2(dot_f32(k, q, 1, 1) * (scale * LOG2E) - lse)
        if diagonal:
            probs = causal(probs, 0.0)
        dv_s[rows, :] += dot_f32(probs.astype(jnp.bfloat16), grad, 1, 0)
        d_probs = dot_f32(v_ref[0, rows, :], grad, 1, 1)
        d_scores = (probs * (d_probs - delta)).astype(jnp.bfloat16)
        dk_s[rows, :] += dot_f32(d_scores, q, 1, 0)
        dq_s[...] += dot_f32(k, d_scores, 0, 0)

    def body(j, carry):
        step(j, False)
        return carry

    lax.fori_loop(0, i, body, 0)
    step(i, True)
    here = pl.ds(pl.multiple_of(i * block, block), block)
    out_ref[0, here, 0:HEAD_DIM] = (jnp.transpose(dq_s[...]) * scale).astype(jnp.bfloat16)

    @pl.when(i == blocks - 1)
    def _():
        out_ref[0, :, HEAD_DIM : 2 * HEAD_DIM] = (dk_s[...] * scale).astype(jnp.bfloat16)
        out_ref[0, :, 2 * HEAD_DIM : 3 * HEAD_DIM] = dv_s[...].astype(jnp.bfloat16)


def attn_bwd(packed, attended, grad, lse):
    count, length, _ = packed.shape
    block = min(ATTN_BLOCK, length)
    rows = pl.BlockSpec((1, block, HEAD_DIM), lambda b, i: (b, i, 0))
    return pl.pallas_call(
        functools.partial(
            attn_bwd_kernel,
            block=block,
            scale=1.0 / math.sqrt(HEAD_DIM),
            blocks=length // block,
        ),
        grid=(count, length // block),
        in_specs=[
            rows,
            pl.BlockSpec((1, length, HEAD_DIM), lambda b, i: (b, 0, 1)),
            pl.BlockSpec((1, length, HEAD_DIM), lambda b, i: (b, 0, 2)),
            rows,
            rows,
            pl.BlockSpec((1, 1, block), lambda b, i: (b, 0, i)),
        ],
        out_specs=pl.BlockSpec((1, length, 3 * HEAD_DIM), lambda b, i: (b, 0, 0)),
        out_shape=jax.ShapeDtypeStruct((count, length, 3 * HEAD_DIM), jnp.bfloat16),
        scratch_shapes=[
            pltpu.VMEM((length, HEAD_DIM), jnp.float32),
            pltpu.VMEM((length, HEAD_DIM), jnp.float32),
            pltpu.VMEM((HEAD_DIM, block), jnp.float32),
        ],
        cost_estimate=pl.CostEstimate(
            flops=5 * count * length * length * HEAD_DIM,
            bytes_accessed=18 * count * length * HEAD_DIM,
            transcendentals=count * length * length // 2,
        ),
        name="attn_bwd",
    )(packed, packed, packed, attended, grad, lse)


def to_heads(values_in, ctx_size):
    seqs, span, heads, width = values_in.shape
    each = heads // ctx_size
    parts = values_in.reshape(seqs, span, ctx_size, each, width).transpose(2, 0, 3, 1, 4)
    parts = lax.all_to_all(parts, "ctx", 0, 0, tiled=True)
    return parts.transpose(1, 2, 0, 3, 4).reshape(seqs * each, ctx_size * span, width)


def to_positions(values_in, seqs, ctx_size):
    count, length, width = values_in.shape
    each, span = count // seqs, length // ctx_size
    parts = values_in.reshape(seqs, each, ctx_size, span, width).transpose(2, 0, 1, 3, 4)
    parts = lax.all_to_all(parts, "ctx", 0, 0, tiled=True)
    return parts.transpose(1, 3, 0, 2, 4).reshape(seqs, span, ctx_size * each, width)


def heads_to_own(values_in, seqs, ctx_size, tensor):
    count, length, width = values_in.shape
    each, span = count // seqs, length // ctx_size
    parts = values_in.reshape(seqs, each, ctx_size, span, width).transpose(2, 0, 3, 1, 4)
    parts = parts.reshape(ctx_size * tensor, seqs * span // tensor, each * width)
    parts = lax.all_to_all(parts, ("ctx", "tp"), 0, 0, tiled=True)
    parts = parts.reshape(ctx_size, tensor, -1, each * width).transpose(2, 1, 0, 3)
    return parts.reshape(seqs * span // tensor, tensor * ctx_size * each * width)


def own_to_heads(values_in, seqs, ctx_size, tensor, width):
    own = values_in.shape[0]
    each = values_in.shape[1] // (tensor * ctx_size * width)
    span = own * tensor // seqs
    parts = values_in.reshape(own, tensor, ctx_size, each * width).transpose(2, 1, 0, 3)
    parts = parts.reshape(ctx_size * tensor, own, each * width)
    parts = lax.all_to_all(parts, ("ctx", "tp"), 0, 0, tiled=True)
    parts = parts.reshape(ctx_size, seqs, span, each, width).transpose(1, 3, 0, 2, 4)
    return parts.reshape(seqs * each, ctx_size * span, width)


def tensor_scatter(values_in):
    tensor = lax.axis_size("tp")
    parts = values_in.astype(jnp.bfloat16).reshape(tensor, -1, values_in.shape[1])
    parts = lax.all_to_all(parts, "tp", 0, 0, tiled=True)
    return jnp.sum(parts.astype(jnp.float32), axis=0)


def tensor_gather(values_in):
    tensor = lax.axis_size("tp")
    parts = jnp.broadcast_to(values_in[None], (tensor,) + values_in.shape)
    return lax.all_to_all(parts, "tp", 0, 0, tiled=True)


def tensor_sum(values_in):
    values_in = values_in.astype(jnp.bfloat16)
    total = lax.psum(values_in, "tp")
    return total.astype(jnp.float32)


def gather_rows(values_in):
    return lax.all_gather(values_in, weight_axes, axis=0, tiled=True)


def scatter_rows(values_in):
    values_in = values_in.astype(jnp.bfloat16)
    return lax.psum_scatter(values_in, weight_axes, scatter_dimension=0, tiled=True)


def per_device(
    tokens,
    q_weight,
    k_weight,
    v_weight,
    o_weight,
    gate_weight,
    up_weight,
    down_weight,
    norm_gains,
    cotangent,
):
    seq_count, seq_span, model_width = tokens.shape
    row_count = seq_count * seq_span
    tensor = lax.axis_size("tp")
    ctx_size = lax.axis_size("ctx")
    local_width = model_width // tensor
    hidden = gate_weight.shape[1]
    heads_here = local_width // HEAD_DIM
    feature_start = lax.axis_index("tp") * local_width
    position = lax.axis_index("ctx") * seq_span
    q_shape = (seq_count, seq_span, heads_here, HEAD_DIM)

    w_qkv = gather_rows(jnp.concatenate([q_weight, k_weight, v_weight], axis=1))
    out_rows = tensor_gather(o_weight).transpose(1, 0, 2).reshape(-1, model_width)
    w_out = gather_rows(out_rows)
    w_gate_up = gather_rows(jnp.concatenate([gate_weight, up_weight], axis=1))
    w_down = gather_rows(down_weight)
    gain_table = gather_rows(norm_gains).astype(jnp.float32)
    gain_q = lax.dynamic_slice_in_dim(gain_table[:, 0], feature_start, local_width)
    gain_k = lax.dynamic_slice_in_dim(gain_table[:, 1], feature_start, local_width)
    gain_attn = gain_table[:, 2]
    gain_ffn = gain_table[:, 3]
    inputs = tokens.reshape(row_count, model_width)
    own_count = row_count // tensor
    own_start = lax.axis_index("tp") * own_count
    own_inputs = lax.dynamic_slice_in_dim(inputs, own_start, own_count).astype(jnp.float32)
    cosine_table, sine_table = rope_tables(seq_span, position)

    qkv_proj = jnp.dot(inputs, w_qkv, preferred_element_type=jnp.float32)
    q_proj = qkv_proj[:, :local_width]
    k_proj = qkv_proj[:, local_width : 2 * local_width]
    v_low = qkv_proj[:, 2 * local_width :].astype(jnp.bfloat16)
    q_squares, k_squares = lax.psum(
        (jnp.sum(q_proj * q_proj, axis=1), jnp.sum(k_proj * k_proj, axis=1)), "tp"
    )
    q_rs = lax.rsqrt(q_squares / model_width + norm_eps)[:, None]
    k_rs = lax.rsqrt(k_squares / model_width + norm_eps)[:, None]
    q_rot = rotate((q_proj * q_rs * gain_q).reshape(q_shape), cosine_table, sine_table)
    k_rot = rotate((k_proj * k_rs * gain_k).reshape(q_shape), cosine_table, sine_table)
    packed = to_heads(
        jnp.concatenate(
            [q_rot.astype(jnp.bfloat16), k_rot.astype(jnp.bfloat16), v_low.reshape(q_shape)], axis=-1
        ),
        ctx_size,
    )
    attended, log_total = attn_fwd(packed)
    att_own = heads_to_own(attended, seq_count, ctx_size, tensor)
    branch_a = contract_cols(att_own, w_out)
    a_rs = rms_scale(branch_a)
    middle_own = own_inputs + branch_a * a_rs * gain_attn
    middle_low = tensor_gather(middle_own.astype(jnp.bfloat16)).reshape(row_count, model_width)
    att_low = to_positions(attended, seq_count, ctx_size).reshape(row_count, local_width)
    gate_up = jnp.dot(middle_low, w_gate_up, preferred_element_type=jnp.float32)
    gate_proj = gate_up[:, :hidden]
    up_proj = gate_up[:, hidden:]
    activated = (jax.nn.silu(gate_proj) * up_proj).astype(jnp.bfloat16)
    branch_f = tensor_sum(contract_cols(activated, w_down))
    f_rs = rms_scale(branch_f)
    block_out = (
        (middle_low.astype(jnp.float32) + branch_f * f_rs * gain_ffn)
        .astype(jnp.bfloat16)
        .reshape(seq_count, seq_span, model_width)
    )
    grad_out = cotangent.reshape(row_count, model_width).astype(jnp.float32)
    ffn_gain_part = jnp.sum(grad_out * branch_f * f_rs, axis=0)
    ffn_dot = jnp.sum(grad_out * gain_ffn * branch_f, axis=1, keepdims=True)
    d_branch_f = norm_backward(grad_out, branch_f, f_rs, gain_ffn, ffn_dot, model_width).astype(
        jnp.bfloat16
    )
    down_part = contract_rows(d_branch_f, activated)
    down_grad = scatter_rows(down_part).astype(jnp.float32)
    d_act = jnp.dot(d_branch_f, w_down, preferred_element_type=jnp.float32)
    sigmoid_gate = jax.nn.sigmoid(gate_proj)
    d_gate = (d_act * up_proj * sigmoid_gate * (1.0 + gate_proj * (1.0 - sigmoid_gate))).astype(
        jnp.bfloat16
    )
    d_up = (d_act * gate_proj * sigmoid_gate).astype(jnp.bfloat16)
    d_gate_up = jnp.concatenate([d_gate, d_up], axis=1)
    own_grad_out = lax.dynamic_slice_in_dim(
        cotangent.reshape(row_count, model_width), own_start, own_count
    ).astype(jnp.float32)
    d_middle = own_grad_out + tensor_scatter(contract_cols(d_gate_up, w_gate_up))
    gate_up_part = contract_rows(middle_low, d_gate_up)
    gate_up_grad = scatter_rows(gate_up_part).astype(jnp.float32)
    attn_gain_part = jnp.sum(d_middle * branch_a * a_rs, axis=0)
    attn_dot = jnp.sum(d_middle * gain_attn * branch_a, axis=1, keepdims=True)
    d_branch_own = norm_backward(d_middle, branch_a, a_rs, gain_attn, attn_dot, model_width).astype(
        jnp.bfloat16
    )
    d_att_own = jnp.dot(d_branch_own, w_out, preferred_element_type=jnp.float32).astype(jnp.bfloat16)
    d_att = own_to_heads(d_att_own, seq_count, ctx_size, tensor, HEAD_DIM)
    d_branch_own, d_att = lax.optimization_barrier((d_branch_own, d_att))
    d_branch_a = tensor_gather(d_branch_own).reshape(row_count, model_width)
    out_part = contract_rows(d_branch_a, att_low)
    out_grad = scatter_rows(out_part).astype(jnp.float32)
    d_packed = to_positions(
        attn_bwd(packed, attended, d_att, log_total),
        seq_count,
        ctx_size,
    )
    d_q_rot = d_packed[..., :HEAD_DIM].astype(jnp.float32)
    d_k_rot = d_packed[..., HEAD_DIM : 2 * HEAD_DIM].astype(jnp.float32)
    d_value = d_packed[..., 2 * HEAD_DIM :].reshape(row_count, local_width)
    d_q_norm = unrotate(d_q_rot, cosine_table, sine_table).reshape(row_count, local_width)
    d_k_norm = unrotate(d_k_rot, cosine_table, sine_table).reshape(row_count, local_width)
    query_gain_part = jnp.sum(d_q_norm * q_proj * q_rs, axis=0)
    key_gain_part = jnp.sum(d_k_norm * k_proj * k_rs, axis=0)
    pre_gains = lax.dynamic_update_slice(
        jnp.zeros((2, model_width), jnp.float32),
        jnp.stack([query_gain_part, key_gain_part]),
        (0, feature_start),
    )
    is_first = lax.axis_index("tp") == 0
    post_gains = jnp.stack([attn_gain_part, jnp.where(is_first, ffn_gain_part, 0.0)])
    query_dot, key_dot = lax.psum(
        (jnp.sum(d_q_norm * gain_q * q_proj, axis=1), jnp.sum(d_k_norm * gain_k * k_proj, axis=1)),
        "tp",
    )
    d_query = norm_backward(d_q_norm, q_proj, q_rs, gain_q, query_dot[:, None], model_width)
    d_key = norm_backward(d_k_norm, k_proj, k_rs, gain_k, key_dot[:, None], model_width)
    d_qkv = jnp.concatenate(
        [d_query.astype(jnp.bfloat16), d_key.astype(jnp.bfloat16), d_value], axis=1
    )
    token_own = d_middle + tensor_scatter(contract_cols(d_qkv, w_qkv))
    token_grad = (
        tensor_gather(token_own.astype(jnp.bfloat16))
        .astype(jnp.float32)
        .reshape(seq_count, seq_span, model_width)
    )
    gain_part, d_qkv = lax.optimization_barrier(
        (jnp.concatenate([pre_gains, post_gains], axis=0), d_qkv)
    )
    gain_sum = lax.psum(gain_part, "tp")
    gain_high = gain_sum.astype(jnp.bfloat16)
    gain_rest = (gain_sum - gain_high.astype(jnp.float32)).astype(jnp.bfloat16)
    gain_terms = jnp.concatenate([gain_high, gain_rest], axis=0).T
    gain_terms = jnp.pad(gain_terms, ((0, 0), (0, HEAD_DIM - gain_terms.shape[1])))
    qkv_part = contract_rows(inputs, d_qkv).astype(jnp.bfloat16)
    last_grad = scatter_rows(jnp.concatenate([qkv_part, gain_terms], axis=1)).astype(jnp.float32)
    qkv_grad = last_grad[:, : 3 * local_width]
    gain_grad = (
        last_grad[:, 3 * local_width : 3 * local_width + 4]
        + last_grad[:, 3 * local_width + 4 : 3 * local_width + 8]
    )
    return (
        block_out,
        token_grad,
        qkv_grad[:, :local_width],
        qkv_grad[:, local_width : 2 * local_width],
        qkv_grad[:, 2 * local_width :],
        out_grad,
        gate_up_grad[:, :hidden],
        gate_up_grad[:, hidden:],
        down_grad,
        gain_grad,
    )


def solution(mesh):
    weight_spec = P(weight_axes, "tp")
    token_spec = P("fsdp", "ctx", None)
    return jax.shard_map(
        per_device,
        mesh=mesh,
        in_specs=(token_spec,) + (weight_spec,) * 7 + (P(weight_axes, None), token_spec),
        out_specs=(token_spec, token_spec) + (weight_spec,) * 7 + (P(weight_axes, None),),
        check_vma=False,
    )
```

```python
import functools
import math

import jax
import jax.numpy as jnp
from jax import lax
from jax.experimental import pallas as pl
from jax.experimental.pallas import tpu as pltpu
from jax.sharding import PartitionSpec as P


HEAD_DIM = 128
LOG2E = 1.4426950408889634
ATTN_BLOCK = 512

norm_eps = 1e-06
rope_base = 500000.0
weight_axes = ("fsdp", "ctx")


def rms_scale(values_in):
    return lax.rsqrt(jnp.mean(values_in * values_in, axis=-1, keepdims=True) + norm_eps)


def rope_tables(length, offset):
    half_dim = HEAD_DIM // 2
    frequency = rope_base ** (-(jnp.arange(half_dim, dtype=jnp.float32) * 2.0) / HEAD_DIM)
    angles = (offset + jnp.arange(length, dtype=jnp.int32)).astype(jnp.float32)[
        :, None
    ] * frequency[None, :]
    return (jnp.cos(angles), jnp.sin(angles))


def rotate(values_in, cosine_table, sine_table):
    half_dim = values_in.shape[-1] // 2
    first_half = values_in[..., :half_dim]
    second_half = values_in[..., half_dim:]
    cosine = cosine_table[:, None, :]
    sine_part = sine_table[:, None, :]
    return jnp.concatenate(
        [
            first_half * cosine - second_half * sine_part,
            second_half * cosine + first_half * sine_part,
        ],
        axis=-1,
    )


def unrotate(grad_in, cosine_table, sine_table):
    return rotate(grad_in, cosine_table, -sine_table)


def dot_f32(left, right, left_dim, right_dim):
    return lax.dot_general(
        left,
        right,
        (((left_dim,), (right_dim,)), ((), ())),
        preferred_element_type=jnp.float32,
    )


def contract_rows(left, right):
    return dot_f32(left, right, 0, 0)


def contract_cols(left, right):
    return dot_f32(left, right, 1, 1)


def norm_backward(grad_in, values_in, scale_rows, gain_vec, dot_rows, model_width):
    cubed = scale_rows * scale_rows * scale_rows
    return scale_rows * (grad_in * gain_vec) - values_in * (cubed / model_width) * dot_rows


def causal(values_in, fill):
    keys = lax.broadcasted_iota(jnp.int32, values_in.shape, 0)
    queries = lax.broadcasted_iota(jnp.int32, values_in.shape, 1)
    return jnp.where(keys <= queries, values_in, fill)


def attn_fwd_kernel(q_ref, k_ref, v_ref, out_ref, lse_ref, max_s, sum_s, acc_s, *, block, scale):
    i = pl.program_id(1)
    q = q_ref[0]
    max_s[...] = jnp.full(max_s.shape, -1e30, jnp.float32)
    sum_s[...] = jnp.zeros_like(sum_s)
    acc_s[...] = jnp.zeros_like(acc_s)

    def step(j, diagonal):
        rows = pl.ds(pl.multiple_of(j * block, block), block)
        scores = dot_f32(k_ref[0, rows, :], q, 1, 1) * (scale * LOG2E)
        if diagonal:
            scores = causal(scores, -1e30)
        old_max = max_s[...]
        new_max = jnp.maximum(old_max, jnp.max(scores, axis=0, keepdims=True))
        decay = jnp.exp2(old_max - new_max)
        weights = jnp.exp2(scores - new_max)
        sum_s[...] = sum_s[...] * decay + jnp.sum(weights, axis=0, keepdims=True)
        max_s[...] = new_max
        acc_s[...] = acc_s[...] * decay + dot_f32(
            v_ref[0, rows, :], weights.astype(jnp.bfloat16), 0, 0
        )

    def body(j, carry):
        step(j, False)
        return carry

    lax.fori_loop(0, i, body, 0)
    step(i, True)
    total = sum_s[...]
    out_ref[0] = jnp.transpose(acc_s[...] / total).astype(jnp.bfloat16)
    lse_ref[0] = max_s[...] + jnp.log2(total)


def attn_fwd(packed):
    count, length, _ = packed.shape
    block = min(ATTN_BLOCK, length)
    rows = pl.BlockSpec((1, block, HEAD_DIM), lambda b, i: (b, i, 0))
    return pl.pallas_call(
        functools.partial(attn_fwd_kernel, block=block, scale=1.0 / math.sqrt(HEAD_DIM)),
        grid=(count, length // block),
        in_specs=[
            rows,
            pl.BlockSpec((1, length, HEAD_DIM), lambda b, i: (b, 0, 1)),
            pl.BlockSpec((1, length, HEAD_DIM), lambda b, i: (b, 0, 2)),
        ],
        out_specs=[rows, pl.BlockSpec((1, 1, block), lambda b, i: (b, 0, i))],
        out_shape=[
            jax.ShapeDtypeStruct((count, length, HEAD_DIM), jnp.bfloat16),
            jax.ShapeDtypeStruct((count, 1, length), jnp.float32),
        ],
        scratch_shapes=[
            pltpu.VMEM((1, block), jnp.float32),
            pltpu.VMEM((1, block), jnp.float32),
            pltpu.VMEM((HEAD_DIM, block), jnp.float32),
        ],
        cost_estimate=pl.CostEstimate(
            flops=2 * count * length * length * HEAD_DIM,
            bytes_accessed=10 * count * length * HEAD_DIM,
            transcendentals=count * length * length // 2,
        ),
        name="attn_fwd",
    )(packed, packed, packed)


def attn_bwd_kernel(
    q_ref, k_ref, v_ref, att_ref, grad_ref, lse_ref, out_ref, dk_s, dv_s, dq_s, *, block, scale, blocks
):
    i = pl.program_id(1)

    @pl.when(i == 0)
    def _():
        dk_s[...] = jnp.zeros_like(dk_s)
        dv_s[...] = jnp.zeros_like(dv_s)

    q = q_ref[0]
    grad = grad_ref[0]
    lse = lse_ref[0]
    delta = jnp.sum(
        jnp.transpose(grad.astype(jnp.float32) * att_ref[0].astype(jnp.float32)),
        axis=0,
        keepdims=True,
    )
    dq_s[...] = jnp.zeros_like(dq_s)

    def step(j, diagonal):
        rows = pl.ds(pl.multiple_of(j * block, block), block)
        k = k_ref[0, rows, :]
        probs = jnp.exp2(dot_f32(k, q, 1, 1) * (scale * LOG2E) - lse)
        if diagonal:
            probs = causal(probs, 0.0)
        dv_s[rows, :] += dot_f32(probs.astype(jnp.bfloat16), grad, 1, 0)
        d_probs = dot_f32(v_ref[0, rows, :], grad, 1, 1)
        d_scores = (probs * (d_probs - delta)).astype(jnp.bfloat16)
        dk_s[rows, :] += dot_f32(d_scores, q, 1, 0)
        dq_s[...] += dot_f32(k, d_scores, 0, 0)

    def body(j, carry):
        step(j, False)
        return carry

    lax.fori_loop(0, i, body, 0)
    step(i, True)
    here = pl.ds(pl.multiple_of(i * block, block), block)
    out_ref[0, here, 0:HEAD_DIM] = (jnp.transpose(dq_s[...]) * scale).astype(jnp.bfloat16)

    @pl.when(i == blocks - 1)
    def _():
        out_ref[0, :, HEAD_DIM : 2 * HEAD_DIM] = (dk_s[...] * scale).astype(jnp.bfloat16)
        out_ref[0, :, 2 * HEAD_DIM : 3 * HEAD_DIM] = dv_s[...].astype(jnp.bfloat16)


def attn_bwd(packed, attended, grad, lse):
    count, length, _ = packed.shape
    block = min(ATTN_BLOCK, length)
    rows = pl.BlockSpec((1, block, HEAD_DIM), lambda b, i: (b, i, 0))
    return pl.pallas_call(
        functools.partial(
            attn_bwd_kernel,
            block=block,
            scale=1.0 / math.sqrt(HEAD_DIM),
            blocks=length // block,
        ),
        grid=(count, length // block),
        in_specs=[
            rows,
            pl.BlockSpec((1, length, HEAD_DIM), lambda b, i: (b, 0, 1)),
            pl.BlockSpec((1, length, HEAD_DIM), lambda b, i: (b, 0, 2)),
            rows,
            rows,
            pl.BlockSpec((1, 1, block), lambda b, i: (b, 0, i)),
        ],
        out_specs=pl.BlockSpec((1, length, 3 * HEAD_DIM), lambda b, i: (b, 0, 0)),
        out_shape=jax.ShapeDtypeStruct((count, length, 3 * HEAD_DIM), jnp.bfloat16),
        scratch_shapes=[
            pltpu.VMEM((length, HEAD_DIM), jnp.float32),
            pltpu.VMEM((length, HEAD_DIM), jnp.float32),
            pltpu.VMEM((HEAD_DIM, block), jnp.float32),
        ],
        cost_estimate=pl.CostEstimate(
            flops=5 * count * length * length * HEAD_DIM,
            bytes_accessed=18 * count * length * HEAD_DIM,
            transcendentals=count * length * length // 2,
        ),
        name="attn_bwd",
    )(packed, packed, packed, attended, grad, lse)


def to_heads(values_in, ctx_size):
    seqs, span, heads, width = values_in.shape
    each = heads // ctx_size
    parts = values_in.reshape(seqs, span, ctx_size, each, width).transpose(2, 0, 3, 1, 4)
    parts = lax.all_to_all(parts, "ctx", 0, 0, tiled=True)
    return parts.transpose(1, 2, 0, 3, 4).reshape(seqs * each, ctx_size * span, width)


def to_positions(values_in, seqs, ctx_size):
    count, length, width = values_in.shape
    each, span = count // seqs, length // ctx_size
    parts = values_in.reshape(seqs, each, ctx_size, span, width).transpose(2, 0, 1, 3, 4)
    parts = lax.all_to_all(parts, "ctx", 0, 0, tiled=True)
    return parts.transpose(1, 3, 0, 2, 4).reshape(seqs, span, ctx_size * each, width)


def heads_to_own(values_in, seqs, ctx_size, tensor):
    count, length, width = values_in.shape
    each, span = count // seqs, length // ctx_size
    parts = values_in.reshape(seqs, each, ctx_size, span, width).transpose(2, 0, 3, 1, 4)
    parts = parts.reshape(ctx_size * tensor, seqs * span // tensor, each * width)
    parts = lax.all_to_all(parts, ("ctx", "tp"), 0, 0, tiled=True)
    parts = parts.reshape(ctx_size, tensor, -1, each * width).transpose(2, 1, 0, 3)
    return parts.reshape(seqs * span // tensor, tensor * ctx_size * each * width)


def own_to_heads(values_in, seqs, ctx_size, tensor, width):
    own = values_in.shape[0]
    each = values_in.shape[1] // (tensor * ctx_size * width)
    span = own * tensor // seqs
    parts = values_in.reshape(own, tensor, ctx_size, each * width).transpose(2, 1, 0, 3)
    parts = parts.reshape(ctx_size * tensor, own, each * width)
    parts = lax.all_to_all(parts, ("ctx", "tp"), 0, 0, tiled=True)
    parts = parts.reshape(ctx_size, seqs, span, each, width).transpose(1, 3, 0, 2, 4)
    return parts.reshape(seqs * each, ctx_size * span, width)


def tensor_scatter(values_in):
    tensor = lax.axis_size("tp")
    parts = values_in.astype(jnp.bfloat16).reshape(tensor, -1, values_in.shape[1])
    parts = lax.all_to_all(parts, "tp", 0, 0, tiled=True)
    return jnp.sum(parts.astype(jnp.float32), axis=0)


def tensor_gather(values_in):
    tensor = lax.axis_size("tp")
    parts = jnp.broadcast_to(values_in[None], (tensor,) + values_in.shape)
    return lax.all_to_all(parts, "tp", 0, 0, tiled=True)


def tensor_sum(values_in):
    values_in = values_in.astype(jnp.bfloat16)
    total = lax.psum(values_in, "tp")
    return total.astype(jnp.float32)


def gather_rows(values_in):
    return lax.all_gather(values_in, weight_axes, axis=0, tiled=True)


def scatter_rows(values_in):
    values_in = values_in.astype(jnp.bfloat16)
    return lax.psum_scatter(values_in, weight_axes, scatter_dimension=0, tiled=True)


def per_device(
    tokens,
    q_weight,
    k_weight,
    v_weight,
    o_weight,
    gate_weight,
    up_weight,
    down_weight,
    norm_gains,
    cotangent,
):
    seq_count, seq_span, model_width = tokens.shape
    row_count = seq_count * seq_span
    tensor = lax.axis_size("tp")
    ctx_size = lax.axis_size("ctx")
    local_width = model_width // tensor
    hidden = gate_weight.shape[1]
    heads_here = local_width // HEAD_DIM
    feature_start = lax.axis_index("tp") * local_width
    position = lax.axis_index("ctx") * seq_span
    q_shape = (seq_count, seq_span, heads_here, HEAD_DIM)

    w_qkv = gather_rows(jnp.concatenate([q_weight, k_weight, v_weight], axis=1))
    out_rows = tensor_gather(o_weight).transpose(1, 0, 2).reshape(-1, model_width)
    w_middle = gather_rows(jnp.concatenate([out_rows, gate_weight, up_weight], axis=1))
    w_out = w_middle[:, :model_width]
    w_gate_up = w_middle[:, model_width:]
    w_down = gather_rows(down_weight)
    gain_table = gather_rows(norm_gains).astype(jnp.float32)
    gain_q = lax.dynamic_slice_in_dim(gain_table[:, 0], feature_start, local_width)
    gain_k = lax.dynamic_slice_in_dim(gain_table[:, 1], feature_start, local_width)
    gain_attn = gain_table[:, 2]
    gain_ffn = gain_table[:, 3]
    inputs = tokens.reshape(row_count, model_width)
    own_count = row_count // tensor
    own_start = lax.axis_index("tp") * own_count
    own_inputs = lax.dynamic_slice_in_dim(inputs, own_start, own_count).astype(jnp.float32)
    cosine_table, sine_table = rope_tables(seq_span, position)

    qkv_proj = jnp.dot(inputs, w_qkv, preferred_element_type=jnp.float32)
    q_proj = qkv_proj[:, :local_width]
    k_proj = qkv_proj[:, local_width : 2 * local_width]
    v_low = qkv_proj[:, 2 * local_width :].astype(jnp.bfloat16)
    q_squares, k_squares = lax.psum(
        (jnp.sum(q_proj * q_proj, axis=1), jnp.sum(k_proj * k_proj, axis=1)), "tp"
    )
    q_rs = lax.rsqrt(q_squares / model_width + norm_eps)[:, None]
    k_rs = lax.rsqrt(k_squares / model_width + norm_eps)[:, None]
    q_rot = rotate((q_proj * q_rs * gain_q).reshape(q_shape), cosine_table, sine_table)
    k_rot = rotate((k_proj * k_rs * gain_k).reshape(q_shape), cosine_table, sine_table)
    packed = to_heads(
        jnp.concatenate(
            [q_rot.astype(jnp.bfloat16), k_rot.astype(jnp.bfloat16), v_low.reshape(q_shape)], axis=-1
        ),
        ctx_size,
    )
    attended, log_total = attn_fwd(packed)
    att_own = heads_to_own(attended, seq_count, ctx_size, tensor)
    branch_a = contract_cols(att_own, w_out)
    a_rs = rms_scale(branch_a)
    middle_own = own_inputs + branch_a * a_rs * gain_attn
    middle_low = tensor_gather(middle_own.astype(jnp.bfloat16)).reshape(row_count, model_width)
    att_low = to_positions(attended, seq_count, ctx_size).reshape(row_count, local_width)
    gate_up = jnp.dot(middle_low, w_gate_up, preferred_element_type=jnp.float32)
    gate_proj = gate_up[:, :hidden]
    up_proj = gate_up[:, hidden:]
    activated = (jax.nn.silu(gate_proj) * up_proj).astype(jnp.bfloat16)
    branch_f = tensor_sum(contract_cols(activated, w_down))
    f_rs = rms_scale(branch_f)
    block_out = (
        (middle_low.astype(jnp.float32) + branch_f * f_rs * gain_ffn)
        .astype(jnp.bfloat16)
        .reshape(seq_count, seq_span, model_width)
    )
    grad_out = cotangent.reshape(row_count, model_width).astype(jnp.float32)
    ffn_gain_part = jnp.sum(grad_out * branch_f * f_rs, axis=0)
    ffn_dot = jnp.sum(grad_out * gain_ffn * branch_f, axis=1, keepdims=True)
    d_branch_f = norm_backward(grad_out, branch_f, f_rs, gain_ffn, ffn_dot, model_width).astype(
        jnp.bfloat16
    )
    down_part = contract_rows(d_branch_f, activated)
    down_grad = scatter_rows(down_part).astype(jnp.float32)
    d_act = jnp.dot(d_branch_f, w_down, preferred_element_type=jnp.float32)
    sigmoid_gate = jax.nn.sigmoid(gate_proj)
    d_gate = (d_act * up_proj * sigmoid_gate * (1.0 + gate_proj * (1.0 - sigmoid_gate))).astype(
        jnp.bfloat16
    )
    d_up = (d_act * gate_proj * sigmoid_gate).astype(jnp.bfloat16)
    d_gate_up = jnp.concatenate([d_gate, d_up], axis=1)
    own_grad_out = lax.dynamic_slice_in_dim(
        cotangent.reshape(row_count, model_width), own_start, own_count
    ).astype(jnp.float32)
    d_middle = own_grad_out + tensor_scatter(contract_cols(d_gate_up, w_gate_up))
    gate_up_part = contract_rows(middle_low, d_gate_up)
    gate_up_grad = scatter_rows(gate_up_part).astype(jnp.float32)
    attn_gain_part = jnp.sum(d_middle * branch_a * a_rs, axis=0)
    attn_dot = jnp.sum(d_middle * gain_attn * branch_a, axis=1, keepdims=True)
    d_branch_own = norm_backward(d_middle, branch_a, a_rs, gain_attn, attn_dot, model_width).astype(
        jnp.bfloat16
    )
    d_att_own = jnp.dot(d_branch_own, w_out, preferred_element_type=jnp.float32).astype(jnp.bfloat16)
    d_att = own_to_heads(d_att_own, seq_count, ctx_size, tensor, HEAD_DIM)
    d_branch_own, d_att = lax.optimization_barrier((d_branch_own, d_att))
    d_branch_a = tensor_gather(d_branch_own).reshape(row_count, model_width)
    d_packed = to_positions(
        attn_bwd(packed, attended, d_att, log_total),
        seq_count,
        ctx_size,
    )
    d_q_rot = d_packed[..., :HEAD_DIM].astype(jnp.float32)
    d_k_rot = d_packed[..., HEAD_DIM : 2 * HEAD_DIM].astype(jnp.float32)
    d_value = d_packed[..., 2 * HEAD_DIM :].reshape(row_count, local_width)
    d_q_norm = unrotate(d_q_rot, cosine_table, sine_table).reshape(row_count, local_width)
    d_k_norm = unrotate(d_k_rot, cosine_table, sine_table).reshape(row_count, local_width)
    query_gain_part = jnp.sum(d_q_norm * q_proj * q_rs, axis=0)
    key_gain_part = jnp.sum(d_k_norm * k_proj * k_rs, axis=0)
    pre_gains = lax.dynamic_update_slice(
        jnp.zeros((2, model_width), jnp.float32),
        jnp.stack([query_gain_part, key_gain_part]),
        (0, feature_start),
    )
    is_first = lax.axis_index("tp") == 0
    post_gains = jnp.stack([attn_gain_part, jnp.where(is_first, ffn_gain_part, 0.0)])
    query_dot, key_dot = lax.psum(
        (jnp.sum(d_q_norm * gain_q * q_proj, axis=1), jnp.sum(d_k_norm * gain_k * k_proj, axis=1)),
        "tp",
    )
    d_query = norm_backward(d_q_norm, q_proj, q_rs, gain_q, query_dot[:, None], model_width)
    d_key = norm_backward(d_k_norm, k_proj, k_rs, gain_k, key_dot[:, None], model_width)
    d_qkv = jnp.concatenate(
        [d_query.astype(jnp.bfloat16), d_key.astype(jnp.bfloat16), d_value], axis=1
    )
    gain_part = jnp.concatenate([pre_gains, post_gains], axis=0)
    gain_high = gain_part.astype(jnp.bfloat16)
    gain_rest = (gain_part - gain_high.astype(jnp.float32)).astype(jnp.bfloat16)
    gain_terms = jnp.concatenate([gain_high, gain_rest], axis=0).T
    gain_terms = jnp.pad(gain_terms, ((0, 0), (0, HEAD_DIM - gain_terms.shape[1])))
    out_part = contract_rows(d_branch_a, att_low).astype(jnp.bfloat16)
    out_and_gains = scatter_rows(
        jnp.concatenate([out_part, gain_terms], axis=1)
    ).astype(jnp.float32)
    out_grad = out_and_gains[:, :local_width]
    token_own = d_middle + tensor_scatter(contract_cols(d_qkv, w_qkv))
    qkv_part = contract_rows(inputs, d_qkv)
    qkv_grad = scatter_rows(qkv_part).astype(jnp.float32)
    gain_rows = out_and_gains[:, local_width : local_width + 4] + (
        out_and_gains[:, local_width + 4 : local_width + 8]
    )
    token_low = tensor_gather(token_own.astype(jnp.bfloat16))
    token_grad = token_low.astype(jnp.float32).reshape(seq_count, seq_span, model_width)
    gain_rows, _ = lax.optimization_barrier((gain_rows, token_low))
    gain_grad = lax.psum(gain_rows, "tp")
    return (
        block_out,
        token_grad,
        qkv_grad[:, :local_width],
        qkv_grad[:, local_width : 2 * local_width],
        qkv_grad[:, 2 * local_width :],
        out_grad,
        gate_up_grad[:, :hidden],
        gate_up_grad[:, hidden:],
        down_grad,
        gain_grad,
    )


def solution(mesh):
    weight_spec = P(weight_axes, "tp")
    token_spec = P("fsdp", "ctx", None)
    return jax.shard_map(
        per_device,
        mesh=mesh,
        in_specs=(token_spec,) + (weight_spec,) * 7 + (P(weight_axes, None), token_spec),
        out_specs=(token_spec, token_spec) + (weight_spec,) * 7 + (P(weight_axes, None),),
        check_vma=False,
    )
```

```python
import functools
import math

import jax
import jax.numpy as jnp
from jax import lax
from jax.experimental import pallas as pl
from jax.experimental.pallas import tpu as pltpu
from jax.sharding import PartitionSpec as P


HEAD_DIM = 128
LOG2E = 1.4426950408889634
ATTN_BLOCK = 512

norm_eps = 1e-06
rope_base = 500000.0
weight_axes = ("fsdp", "ctx")


def rms_scale(values_in):
    return lax.rsqrt(jnp.mean(values_in * values_in, axis=-1, keepdims=True) + norm_eps)


def rope_tables(length, offset):
    half_dim = HEAD_DIM // 2
    frequency = rope_base ** (-(jnp.arange(half_dim, dtype=jnp.float32) * 2.0) / HEAD_DIM)
    angles = (offset + jnp.arange(length, dtype=jnp.int32)).astype(jnp.float32)[
        :, None
    ] * frequency[None, :]
    return (jnp.cos(angles), jnp.sin(angles))


def rotate(values_in, cosine_table, sine_table):
    half_dim = values_in.shape[-1] // 2
    first_half = values_in[..., :half_dim]
    second_half = values_in[..., half_dim:]
    cosine = cosine_table[:, None, :]
    sine_part = sine_table[:, None, :]
    return jnp.concatenate(
        [
            first_half * cosine - second_half * sine_part,
            second_half * cosine + first_half * sine_part,
        ],
        axis=-1,
    )


def unrotate(grad_in, cosine_table, sine_table):
    return rotate(grad_in, cosine_table, -sine_table)


def dot_f32(left, right, left_dim, right_dim):
    return lax.dot_general(
        left,
        right,
        (((left_dim,), (right_dim,)), ((), ())),
        preferred_element_type=jnp.float32,
    )


def contract_rows(left, right):
    return dot_f32(left, right, 0, 0)


def contract_cols(left, right):
    return dot_f32(left, right, 1, 1)


def norm_backward(grad_in, values_in, scale_rows, gain_vec, dot_rows, model_width):
    cubed = scale_rows * scale_rows * scale_rows
    return scale_rows * (grad_in * gain_vec) - values_in * (cubed / model_width) * dot_rows


def causal(values_in, fill):
    keys = lax.broadcasted_iota(jnp.int32, values_in.shape, 0)
    queries = lax.broadcasted_iota(jnp.int32, values_in.shape, 1)
    return jnp.where(keys <= queries, values_in, fill)


def attn_fwd_kernel(q_ref, k_ref, v_ref, out_ref, lse_ref, max_s, sum_s, acc_s, *, block, scale):
    i = pl.program_id(1)
    q = q_ref[0]
    max_s[...] = jnp.full(max_s.shape, -1e30, jnp.float32)
    sum_s[...] = jnp.zeros_like(sum_s)
    acc_s[...] = jnp.zeros_like(acc_s)

    def step(j, diagonal):
        rows = pl.ds(pl.multiple_of(j * block, block), block)
        scores = dot_f32(k_ref[0, rows, :], q, 1, 1) * (scale * LOG2E)
        if diagonal:
            scores = causal(scores, -1e30)
        old_max = max_s[...]
        new_max = jnp.maximum(old_max, jnp.max(scores, axis=0, keepdims=True))
        decay = jnp.exp2(old_max - new_max)
        weights = jnp.exp2(scores - new_max)
        sum_s[...] = sum_s[...] * decay + jnp.sum(weights, axis=0, keepdims=True)
        max_s[...] = new_max
        acc_s[...] = acc_s[...] * decay + dot_f32(
            v_ref[0, rows, :], weights.astype(jnp.bfloat16), 0, 0
        )

    def body(j, carry):
        step(j, False)
        return carry

    lax.fori_loop(0, i, body, 0)
    step(i, True)
    total = sum_s[...]
    out_ref[0] = jnp.transpose(acc_s[...] / total).astype(jnp.bfloat16)
    lse_ref[0] = max_s[...] + jnp.log2(total)


def attn_fwd(packed):
    count, length, _ = packed.shape
    block = min(ATTN_BLOCK, length)
    rows = pl.BlockSpec((1, block, HEAD_DIM), lambda b, i: (b, i, 0))
    return pl.pallas_call(
        functools.partial(attn_fwd_kernel, block=block, scale=1.0 / math.sqrt(HEAD_DIM)),
        grid=(count, length // block),
        in_specs=[
            rows,
            pl.BlockSpec((1, length, HEAD_DIM), lambda b, i: (b, 0, 1)),
            pl.BlockSpec((1, length, HEAD_DIM), lambda b, i: (b, 0, 2)),
        ],
        out_specs=[rows, pl.BlockSpec((1, 1, block), lambda b, i: (b, 0, i))],
        out_shape=[
            jax.ShapeDtypeStruct((count, length, HEAD_DIM), jnp.bfloat16),
            jax.ShapeDtypeStruct((count, 1, length), jnp.float32),
        ],
        scratch_shapes=[
            pltpu.VMEM((1, block), jnp.float32),
            pltpu.VMEM((1, block), jnp.float32),
            pltpu.VMEM((HEAD_DIM, block), jnp.float32),
        ],
        cost_estimate=pl.CostEstimate(
            flops=2 * count * length * length * HEAD_DIM,
            bytes_accessed=10 * count * length * HEAD_DIM,
            transcendentals=count * length * length // 2,
        ),
        name="attn_fwd",
    )(packed, packed, packed)


def attn_bwd_kernel(
    q_ref, k_ref, v_ref, att_ref, grad_ref, lse_ref, out_ref, dk_s, dv_s, dq_s, *, block, scale, blocks
):
    i = pl.program_id(1)

    @pl.when(i == 0)
    def _():
        dk_s[...] = jnp.zeros_like(dk_s)
        dv_s[...] = jnp.zeros_like(dv_s)

    q = q_ref[0]
    grad = grad_ref[0]
    lse = lse_ref[0]
    delta = jnp.sum(
        jnp.transpose(grad.astype(jnp.float32) * att_ref[0].astype(jnp.float32)),
        axis=0,
        keepdims=True,
    )
    dq_s[...] = jnp.zeros_like(dq_s)

    def step(j, diagonal):
        rows = pl.ds(pl.multiple_of(j * block, block), block)
        k = k_ref[0, rows, :]
        probs = jnp.exp2(dot_f32(k, q, 1, 1) * (scale * LOG2E) - lse)
        if diagonal:
            probs = causal(probs, 0.0)
        dv_s[rows, :] += dot_f32(probs.astype(jnp.bfloat16), grad, 1, 0)
        d_probs = dot_f32(v_ref[0, rows, :], grad, 1, 1)
        d_scores = (probs * (d_probs - delta)).astype(jnp.bfloat16)
        dk_s[rows, :] += dot_f32(d_scores, q, 1, 0)
        dq_s[...] += dot_f32(k, d_scores, 0, 0)

    def body(j, carry):
        step(j, False)
        return carry

    lax.fori_loop(0, i, body, 0)
    step(i, True)
    here = pl.ds(pl.multiple_of(i * block, block), block)
    out_ref[0, here, 0:HEAD_DIM] = (jnp.transpose(dq_s[...]) * scale).astype(jnp.bfloat16)

    @pl.when(i == blocks - 1)
    def _():
        out_ref[0, :, HEAD_DIM : 2 * HEAD_DIM] = (dk_s[...] * scale).astype(jnp.bfloat16)
        out_ref[0, :, 2 * HEAD_DIM : 3 * HEAD_DIM] = dv_s[...].astype(jnp.bfloat16)


def attn_bwd(packed, attended, grad, lse):
    count, length, _ = packed.shape
    block = min(ATTN_BLOCK, length)
    rows = pl.BlockSpec((1, block, HEAD_DIM), lambda b, i: (b, i, 0))
    return pl.pallas_call(
        functools.partial(
            attn_bwd_kernel,
            block=block,
            scale=1.0 / math.sqrt(HEAD_DIM),
            blocks=length // block,
        ),
        grid=(count, length // block),
        in_specs=[
            rows,
            pl.BlockSpec((1, length, HEAD_DIM), lambda b, i: (b, 0, 1)),
            pl.BlockSpec((1, length, HEAD_DIM), lambda b, i: (b, 0, 2)),
            rows,
            rows,
            pl.BlockSpec((1, 1, block), lambda b, i: (b, 0, i)),
        ],
        out_specs=pl.BlockSpec((1, length, 3 * HEAD_DIM), lambda b, i: (b, 0, 0)),
        out_shape=jax.ShapeDtypeStruct((count, length, 3 * HEAD_DIM), jnp.bfloat16),
        scratch_shapes=[
            pltpu.VMEM((length, HEAD_DIM), jnp.float32),
            pltpu.VMEM((length, HEAD_DIM), jnp.float32),
            pltpu.VMEM((HEAD_DIM, block), jnp.float32),
        ],
        cost_estimate=pl.CostEstimate(
            flops=5 * count * length * length * HEAD_DIM,
            bytes_accessed=18 * count * length * HEAD_DIM,
            transcendentals=count * length * length // 2,
        ),
        name="attn_bwd",
    )(packed, packed, packed, attended, grad, lse)


def to_heads(values_in, ctx_size):
    seqs, span, heads, width = values_in.shape
    each = heads // ctx_size
    parts = values_in.reshape(seqs, span, ctx_size, each, width).transpose(2, 0, 3, 1, 4)
    parts = lax.all_to_all(parts, "ctx", 0, 0, tiled=True)
    return parts.transpose(1, 2, 0, 3, 4).reshape(seqs * each, ctx_size * span, width)


def to_positions(values_in, seqs, ctx_size):
    count, length, width = values_in.shape
    each, span = count // seqs, length // ctx_size
    parts = values_in.reshape(seqs, each, ctx_size, span, width).transpose(2, 0, 1, 3, 4)
    parts = lax.all_to_all(parts, "ctx", 0, 0, tiled=True)
    return parts.transpose(1, 3, 0, 2, 4).reshape(seqs, span, ctx_size * each, width)


def own_to_heads(values_in, seqs, ctx_size, tensor, width):
    own = values_in.shape[0]
    each = values_in.shape[1] // (tensor * ctx_size * width)
    span = own * tensor // seqs
    parts = values_in.reshape(own, tensor, ctx_size, each * width).transpose(2, 1, 0, 3)
    parts = parts.reshape(ctx_size * tensor, own, each * width)
    parts = lax.all_to_all(parts, ("ctx", "tp"), 0, 0, tiled=True)
    parts = parts.reshape(ctx_size, seqs, span, each, width).transpose(1, 3, 0, 2, 4)
    return parts.reshape(seqs * each, ctx_size * span, width)


def tensor_scatter(values_in):
    tensor = lax.axis_size("tp")
    parts = values_in.astype(jnp.bfloat16).reshape(tensor, -1, values_in.shape[1])
    parts = lax.all_to_all(parts, "tp", 0, 0, tiled=True)
    return jnp.sum(parts.astype(jnp.float32), axis=0)


def tensor_gather(values_in):
    tensor = lax.axis_size("tp")
    parts = jnp.broadcast_to(values_in[None], (tensor,) + values_in.shape)
    return lax.all_to_all(parts, "tp", 0, 0, tiled=True)


def gather_rows(values_in):
    return lax.all_gather(values_in, weight_axes, axis=0, tiled=True)


def scatter_rows(values_in):
    values_in = values_in.astype(jnp.bfloat16)
    return lax.psum_scatter(values_in, weight_axes, scatter_dimension=0, tiled=True)


def per_device(
    tokens,
    q_weight,
    k_weight,
    v_weight,
    o_weight,
    gate_weight,
    up_weight,
    down_weight,
    norm_gains,
    cotangent,
):
    seq_count, seq_span, model_width = tokens.shape
    row_count = seq_count * seq_span
    tensor = lax.axis_size("tp")
    ctx_size = lax.axis_size("ctx")
    local_width = model_width // tensor
    hidden = gate_weight.shape[1]
    heads_here = local_width // HEAD_DIM
    feature_start = lax.axis_index("tp") * local_width
    position = lax.axis_index("ctx") * seq_span
    q_shape = (seq_count, seq_span, heads_here, HEAD_DIM)

    w_qkv = gather_rows(jnp.concatenate([q_weight, k_weight, v_weight], axis=1))
    w_out_here = gather_rows(o_weight)
    w_ffn = gather_rows(jnp.concatenate([gate_weight, up_weight, down_weight], axis=1))
    w_gate_up = w_ffn[:, : 2 * hidden]
    w_down = w_ffn[:, 2 * hidden :]
    out_rows = tensor_gather(o_weight).transpose(1, 0, 2).reshape(-1, model_width)
    w_out = gather_rows(out_rows)
    gain_table = gather_rows(norm_gains).astype(jnp.float32)
    gain_q = lax.dynamic_slice_in_dim(gain_table[:, 0], feature_start, local_width)
    gain_k = lax.dynamic_slice_in_dim(gain_table[:, 1], feature_start, local_width)
    gain_attn = gain_table[:, 2]
    gain_ffn = gain_table[:, 3]
    inputs = tokens.reshape(row_count, model_width)
    own_count = row_count // tensor
    own_start = lax.axis_index("tp") * own_count
    own_inputs = lax.dynamic_slice_in_dim(inputs, own_start, own_count).astype(jnp.float32)
    cosine_table, sine_table = rope_tables(seq_span, position)

    qkv_proj = jnp.dot(inputs, w_qkv, preferred_element_type=jnp.float32)
    q_proj = qkv_proj[:, :local_width]
    k_proj = qkv_proj[:, local_width : 2 * local_width]
    v_low = qkv_proj[:, 2 * local_width :].astype(jnp.bfloat16)
    q_squares, k_squares = lax.psum(
        (jnp.sum(q_proj * q_proj, axis=1), jnp.sum(k_proj * k_proj, axis=1)), "tp"
    )
    q_rs = lax.rsqrt(q_squares / model_width + norm_eps)[:, None]
    k_rs = lax.rsqrt(k_squares / model_width + norm_eps)[:, None]
    q_rot = rotate((q_proj * q_rs * gain_q).reshape(q_shape), cosine_table, sine_table)
    k_rot = rotate((k_proj * k_rs * gain_k).reshape(q_shape), cosine_table, sine_table)
    packed = to_heads(
        jnp.concatenate(
            [q_rot.astype(jnp.bfloat16), k_rot.astype(jnp.bfloat16), v_low.reshape(q_shape)], axis=-1
        ),
        ctx_size,
    )
    attended, log_total = attn_fwd(packed)
    att_low = to_positions(attended, seq_count, ctx_size).reshape(row_count, local_width)

    half_count = own_count // 2
    half_rows = half_count * tensor
    part = contract_cols(att_low, w_out_here).astype(jnp.bfloat16)
    part = part.reshape(tensor, 2, half_count, model_width)
    branch_a = [tensor_scatter(part[:, half].reshape(half_rows, model_width)) for half in range(2)]
    grad_out_rows = cotangent.reshape(tensor, 2, half_count, model_width)
    middle_low, gate_proj, up_proj, activated, branch_f = [], [], [], [], []
    for half in range(2):
        middle = own_inputs[half * half_count : (half + 1) * half_count] + (
            branch_a[half] * rms_scale(branch_a[half]) * gain_attn
        )
        middle_low.append(
            tensor_gather(middle.astype(jnp.bfloat16)).reshape(half_rows, model_width)
        )
        gate_up = jnp.dot(middle_low[half], w_gate_up, preferred_element_type=jnp.float32)
        gate_proj.append(gate_up[:, :hidden])
        up_proj.append(gate_up[:, hidden:])
        activated.append((jax.nn.silu(gate_proj[half]) * up_proj[half]).astype(jnp.bfloat16))
        part = contract_cols(activated[half], w_down)
        branch_f.append(tensor_scatter(part).astype(jnp.bfloat16))
    branch_f = [
        tensor_gather(branch_f[half])
        .reshape(half_rows, model_width)
        .astype(jnp.float32)
        for half in range(2)
    ]
    block_halves, gain_halves, d_branch_f, d_gate_up, d_middle = [], [], [], [], []
    for half in range(2):
        if half:
            branch_f[half], part = lax.optimization_barrier((branch_f[half], part))
        f_rs = rms_scale(branch_f[half])
        block_halves.append(
            (middle_low[half].astype(jnp.float32) + branch_f[half] * f_rs * gain_ffn)
            .astype(jnp.bfloat16)
            .reshape(tensor, 1, half_count, model_width)
        )
        grad_out = grad_out_rows[:, half].reshape(half_rows, model_width).astype(jnp.float32)
        gain_halves.append(jnp.sum(grad_out * branch_f[half] * f_rs, axis=0))
        ffn_dot = jnp.sum(grad_out * gain_ffn * branch_f[half], axis=1, keepdims=True)
        d_branch_f.append(
            norm_backward(grad_out, branch_f[half], f_rs, gain_ffn, ffn_dot, model_width).astype(
                jnp.bfloat16
            )
        )
        d_act = jnp.dot(d_branch_f[half], w_down, preferred_element_type=jnp.float32)
        gate, up = gate_proj[half], up_proj[half]
        sigmoid_gate = jax.nn.sigmoid(gate)
        d_gate = d_act * up * sigmoid_gate * (1.0 + gate * (1.0 - sigmoid_gate))
        d_up = d_act * gate * sigmoid_gate
        d_gate_up.append(
            jnp.concatenate([d_gate.astype(jnp.bfloat16), d_up.astype(jnp.bfloat16)], axis=1)
        )
        part = contract_cols(d_gate_up[half], w_gate_up)
        d_middle.append(tensor_scatter(part))
    block_out = jnp.concatenate(block_halves, axis=1).reshape(seq_count, seq_span, model_width)
    ffn_gain_part = gain_halves[0] + gain_halves[1]
    down_part = contract_rows(jnp.concatenate(d_branch_f), jnp.concatenate(activated))
    down_grad = scatter_rows(down_part).astype(jnp.float32)
    gate_up_part = contract_rows(jnp.concatenate(middle_low), jnp.concatenate(d_gate_up))
    gate_up_grad = scatter_rows(gate_up_part).astype(jnp.float32)
    own_grad_out = lax.dynamic_slice_in_dim(
        cotangent.reshape(row_count, model_width), own_start, own_count
    ).astype(jnp.float32)
    d_middle = own_grad_out + jnp.concatenate(d_middle)
    branch_a = jnp.concatenate(branch_a)
    a_rs = rms_scale(branch_a)
    attn_gain_part = jnp.sum(d_middle * branch_a * a_rs, axis=0)
    attn_dot = jnp.sum(d_middle * gain_attn * branch_a, axis=1, keepdims=True)
    d_branch_own = norm_backward(d_middle, branch_a, a_rs, gain_attn, attn_dot, model_width).astype(
        jnp.bfloat16
    )
    d_att_own = jnp.dot(d_branch_own, w_out, preferred_element_type=jnp.float32).astype(jnp.bfloat16)
    d_att = own_to_heads(d_att_own, seq_count, ctx_size, tensor, HEAD_DIM)
    d_branch_own, d_att = lax.optimization_barrier((d_branch_own, d_att))
    d_branch_a = tensor_gather(d_branch_own).reshape(row_count, model_width)
    d_packed = to_positions(
        attn_bwd(packed, attended, d_att, log_total),
        seq_count,
        ctx_size,
    )
    d_q_rot = d_packed[..., :HEAD_DIM].astype(jnp.float32)
    d_k_rot = d_packed[..., HEAD_DIM : 2 * HEAD_DIM].astype(jnp.float32)
    d_value = d_packed[..., 2 * HEAD_DIM :].reshape(row_count, local_width)
    d_q_norm = unrotate(d_q_rot, cosine_table, sine_table).reshape(row_count, local_width)
    d_k_norm = unrotate(d_k_rot, cosine_table, sine_table).reshape(row_count, local_width)
    query_gain_part = jnp.sum(d_q_norm * q_proj * q_rs, axis=0)
    key_gain_part = jnp.sum(d_k_norm * k_proj * k_rs, axis=0)
    pre_gains = lax.dynamic_update_slice(
        jnp.zeros((2, model_width), jnp.float32),
        jnp.stack([query_gain_part, key_gain_part]),
        (0, feature_start),
    )
    is_first = lax.axis_index("tp") == 0
    post_gains = jnp.stack([attn_gain_part, jnp.where(is_first, ffn_gain_part, 0.0)])
    query_dot, key_dot = lax.psum(
        (jnp.sum(d_q_norm * gain_q * q_proj, axis=1), jnp.sum(d_k_norm * gain_k * k_proj, axis=1)),
        "tp",
    )
    d_query = norm_backward(d_q_norm, q_proj, q_rs, gain_q, query_dot[:, None], model_width)
    d_key = norm_backward(d_k_norm, k_proj, k_rs, gain_k, key_dot[:, None], model_width)
    d_qkv = jnp.concatenate(
        [d_query.astype(jnp.bfloat16), d_key.astype(jnp.bfloat16), d_value], axis=1
    )
    out_part = contract_rows(d_branch_a, att_low)
    out_grad = scatter_rows(out_part).astype(jnp.float32)
    gain_part = jnp.concatenate([pre_gains, post_gains], axis=0)
    gain_high = gain_part.astype(jnp.bfloat16)
    gain_rest = (gain_part - gain_high.astype(jnp.float32)).astype(jnp.bfloat16)
    gain_terms = jnp.concatenate([gain_high, gain_rest], axis=0).T
    gain_terms = jnp.pad(gain_terms, ((0, 0), (0, HEAD_DIM - gain_terms.shape[1])))
    token_own = d_middle + tensor_scatter(contract_cols(d_qkv, w_qkv))
    qkv_part = contract_rows(inputs, d_qkv).astype(jnp.bfloat16)
    last_grad = scatter_rows(jnp.concatenate([qkv_part, gain_terms], axis=1)).astype(jnp.float32)
    qkv_width = 3 * local_width
    qkv_grad = last_grad[:, :qkv_width]
    gain_rows = last_grad[:, qkv_width : qkv_width + 4] + last_grad[:, qkv_width + 4 : qkv_width + 8]
    token_low = tensor_gather(token_own.astype(jnp.bfloat16))
    token_grad = token_low.astype(jnp.float32).reshape(seq_count, seq_span, model_width)
    gain_rows, _ = lax.optimization_barrier((gain_rows, token_low))
    gain_grad = lax.psum(gain_rows, "tp")
    return (
        block_out,
        token_grad,
        qkv_grad[:, :local_width],
        qkv_grad[:, local_width : 2 * local_width],
        qkv_grad[:, 2 * local_width :],
        out_grad,
        gate_up_grad[:, :hidden],
        gate_up_grad[:, hidden:],
        down_grad,
        gain_grad,
    )


def solution(mesh):
    weight_spec = P(weight_axes, "tp")
    token_spec = P("fsdp", "ctx", None)
    return jax.shard_map(
        per_device,
        mesh=mesh,
        in_specs=(token_spec,) + (weight_spec,) * 7 + (P(weight_axes, None), token_spec),
        out_specs=(token_spec, token_spec) + (weight_spec,) * 7 + (P(weight_axes, None),),
        check_vma=False,
    )
```
